32 devices in a mesh: tm: 8 (over y, x, core), lat: 4 (over z).
Axes of the slice: x: 2, y: 2, z: 4, core: 2. Of those that a mesh axis runs over, the one named last changes fastest.
Arguments:
- incr_static: float32 [8, 32, 192, 128], P('tm', 'lat'), may hold values from -6 to 6
- ens_pert: bfloat16 [8, 8, 32, 192, 128], P(None, 'tm', 'lat'), may hold values from -0.59765625 to 0.59765625
- ens_weight: float32 [8, 4, 1024], P(None, 'lat', 'tm'), may hold values from -6 to 6
- column_map: int32 [32, 192], P('lat'), may hold values from 0 to 1023
- sub_steps: int32 [8], P('tm'), may hold values from 1 to 4, 24 in all
- diffusion: bfloat16 [8, 32, 192, 128], P('tm', 'lat'), may hold values from 0.0099487305 to 0.23925781
- mode_in: bfloat16 [4, 128, 128], replicated, may hold values from -0.5 to 0.5
- mode_out: bfloat16 [4, 128, 128], replicated, may hold values from -0.25 to 0.25
- model_precision: bfloat16 [8, 32, 192, 128], P('tm', 'lat'), may hold values from 0.099609375 to 1
- obs_precision: bfloat16 [8, 32, 192, 128], P('tm', 'lat'), may hold values from 0.099609375 to 1
- innovation: bfloat16 [8, 32, 192, 128], P('tm', 'lat'), may hold values from -6 to 6
Outputs:
- grad_static: float32 [8, 32, 192, 128], P('tm', 'lat')
- grad_weight: float32 [8, 4, 1024], P(None, 'lat', 'tm')
The draws below stay inside these ranges and needn't reach their ends.
Inputs may be any that keep to these rules, and one draw needn't show every extreme that they name: `column_map`: each cell names one of the 1024 weight columns of its own latitude slab. `sub_steps`: the subwindows' step counts add up to 24.
All inputs are finite; a program needn't handle non-finite values. No bound on the sum of `sub_steps` on one device may be relied on, other than what follows from the above.
Results may differ from the reference program's by a relative error of at most 0.0065.
Values may be sent and summed in bfloat16 or wider, within the bound.
A program may use at most 64 MiB of HBM per device.

```python
import math
import jax
import jax.numpy as jnp
import numpy as np
from jax import lax

LAT_DEV = 8
LON = 192
LEV = 128
MEM = 8
STEPS = 4
SUB = 8
LATS = 32
SLABS = 4
CSLAB = 1024


def place_ends(entries, rng, low, high):
    index_at = [jax.random.randint(jax.random.fold_in(rng, axis), (), 0, length) for axis, length in enumerate(entries.shape)]
    main_axis = entries.shape.index(max(entries.shape))
    neighbour = index_at[:main_axis] + [(index_at[main_axis] + 1) % entries.shape[main_axis]] + index_at[main_axis + 1:]
    return entries.at[tuple(index_at)].set(low).at[tuple(neighbour)].set(high)


def block_scale(rng, dims, pieces, low, largest):
    level, own = 1.0, jax.random.fold_in(rng, 6)
    for axis_at, shards_of in pieces:
        draws = jnp.exp(jax.random.uniform(jax.random.fold_in(own, axis_at), (shards_of,), jnp.float32, low / len(pieces), largest / len(pieces)))
        level = level * jnp.repeat(draws, dims[axis_at] // shards_of).reshape([-1 if axis == axis_at else 1 for axis in range(len(dims))])
    return level


def profile(count, total, limit, skew):
    weights = [(1 << 20) // math.isqrt(standing ** skew) + 1 for standing in range(2, count + 1)]
    surplus, holding = total - limit - (count - 1), [1] * (count - 1)
    while surplus > 0:
        free = [i for i in range(count - 1) if holding[i] < limit]
        whole, left = sum([weights[i] for i in free]), surplus
        for i in free:
            addition = min(limit - holding[i], max(1, left * weights[i] // whole), surplus)
            holding[i] = holding[i] + addition
            surplus = surplus - addition
    return np.array([limit] + holding)


def uneven_parts(rng, count, total, limit, slope):
    if count == 2:
        one = jax.random.randint(rng, (), max(1, total - limit), min(limit, total - 1) + 1)
        return jnp.stack([one, total - one])
    sizes = jnp.asarray(profile(count, total, limit, slope), jnp.int32)
    couples = (count - 1) // 2
    donor, sink = sizes[1:1 + 2 * couples:2], sizes[2:2 + 2 * couples:2]
    margin = jnp.minimum(donor - 1, limit - sink)
    passed = jax.random.randint(jax.random.fold_in(rng, 1), (couples,), 0, 1 << 20) % (margin + 1)
    sizes = sizes.at[1:1 + 2 * couples:2].set(donor - passed).at[2:2 + 2 * couples:2].set(sink + passed)
    return sizes[jax.random.permutation(jax.random.fold_in(rng, 2), count)]


def noise(stream_key, extent, scale, bound, shards=(), held_as=jnp.bfloat16):
    values = jax.random.normal(stream_key, extent, jnp.float32) * scale
    if len(shards) > 0:
        values = block_scale(stream_key, extent, shards, -0.22, 0.18) * values
    return jnp.clip(values, min=-bound, max=bound).astype(held_as)


def setup_inputs(seed: int = 0) -> dict:
    streams_of = jax.random.split(jax.random.key(seed), 12)
    incr_static = noise(streams_of[0], (SUB, LATS, LON, LEV), 1.0, 6.0, ((0, 8), (1, 4)), jnp.float32)
    ens_pert = noise(streams_of[1], (MEM, SUB, LATS, LON, LEV), 0.1, 0.59765625, ((1, 8), (2, 4)))
    ens_weight = noise(streams_of[2], (MEM, SLABS, CSLAB), 1.0, 6.0, ((1, 4), (2, 8)), jnp.float32)
    column_map = place_ends(jax.random.randint(streams_of[3], (LATS, LON), 0, CSLAB), jax.random.fold_in(streams_of[3], 1), 0, CSLAB - 1).astype(jnp.int32)
    sub_steps = uneven_parts(streams_of[4], SUB, 3 * SUB, STEPS, 0).astype(jnp.int32)
    diffusion = jnp.clip(jnp.exp(math.log(0.23925781) - 3.1800967 * jax.random.uniform(streams_of[5], (SUB, LATS, LON, LEV), jnp.float32) ** block_scale(streams_of[5], (SUB, LATS, LON, LEV), ((0, 8), (1, 4)), -0.2, 0.2)), 0.0099487305, 0.23925781).astype(jnp.bfloat16)
    mode_in = noise(streams_of[6], (STEPS, LEV, LEV), LEV ** -0.5, 0.5)
    mode_out = noise(streams_of[7], (STEPS, LEV, LEV), (4 * LEV) ** -0.5, 0.25)
    model_precision = jnp.clip(jnp.exp(math.log(1.0) - 2.306499 * jax.random.uniform(streams_of[8], (SUB, LATS, LON, LEV), jnp.float32) ** block_scale(streams_of[8], (SUB, LATS, LON, LEV), ((0, 8), (1, 4)), -0.2, 0.2)), 0.099609375, 1.0).astype(jnp.bfloat16)
    obs_precision = jnp.clip(jnp.exp(math.log(1.0) - 2.306499 * jax.random.uniform(streams_of[9], (SUB, LATS, LON, LEV), jnp.float32) ** block_scale(streams_of[9], (SUB, LATS, LON, LEV), ((0, 8), (1, 4)), -0.2, 0.2)), 0.099609375, 1.0).astype(jnp.bfloat16)
    innovation = noise(streams_of[10], (SUB, LATS, LON, LEV), 1.0, 6.0, ((0, 8), (1, 4)))
    return {"incr_static": incr_static, "ens_pert": ens_pert, "ens_weight": ens_weight, "column_map": column_map, "sub_steps": sub_steps, "diffusion": diffusion, "mode_in": mode_in, "mode_out": mode_out, "model_precision": model_precision, "obs_precision": obs_precision, "innovation": innovation}


def laplace(state_field):
    padded = jnp.pad(state_field, ((1, 1), (0, 0), (0, 0)))
    return (padded[2:] + padded[:-2] + jnp.roll(state_field, 1, axis=1)
            + jnp.roll(state_field, -1, axis=1) - 4.0 * state_field)


def vertical(smoothed, to_modes, from_modes):
    layout = smoothed.shape
    flat = smoothed.astype(jnp.bfloat16).reshape(-1, layout[-1])
    mode_values = jnp.dot(flat, to_modes, preferred_element_type=jnp.float32).astype(jnp.bfloat16)
    return jnp.dot(mode_values, from_modes, preferred_element_type=jnp.float32).reshape(layout)


def tangent(state_field, diffuse, step_count, mode_in, mode_out):
    for section in range(STEPS):
        smoothed = state_field + diffuse * laplace(state_field)
        advanced = smoothed + vertical(smoothed, mode_in[section], mode_out[section])
        state_field = jnp.where(section < step_count, advanced, state_field)
    return state_field


def adjoint(state_field, diffuse, step_count, mode_in, mode_out):
    for section in reversed(range(STEPS)):
        coupled = state_field + vertical(state_field, mode_out[section].T, mode_in[section].T)
        advanced = coupled + laplace(diffuse * coupled)
        state_field = jnp.where(section < step_count, advanced, state_field)
    return state_field


def reference(incr_static, ens_pert, ens_weight, column_map, sub_steps, diffusion, mode_in, mode_out,
              model_precision, obs_precision, innovation):
    row_slab = (jnp.arange(LATS, dtype=jnp.int32) // LAT_DEV).astype(jnp.int32)
    member_weight = jnp.take_along_axis(ens_weight[:, row_slab, :], column_map[None], axis=2)
    segment_ids = (row_slab[:, None] * CSLAB + column_map).reshape(-1)

    def start_of(window):
        pert_here = lax.dynamic_index_in_dim(ens_pert, window, 1, keepdims=False)
        return incr_static[window] + jnp.sum(pert_here.astype(jnp.float32) * member_weight[..., None], axis=0)

    def run(window):
        return tangent(start_of(window), diffusion[window].astype(jnp.float32), sub_steps[window], mode_in, mode_out)

    windows = jnp.arange(SUB, dtype=jnp.int32)
    end_state = lax.map(run, windows)

    def jump_of(window):
        earlier = lax.dynamic_index_in_dim(end_state, jnp.maximum(window - 1, 0), 0, keepdims=False)
        earlier = jnp.where(window > 0, earlier, jnp.zeros_like(earlier))
        return model_precision[window].astype(jnp.float32) * (start_of(window) - earlier)

    def gradient_of(window):
        own_jump = jump_of(window)
        next_jump = jump_of(jnp.minimum(window + 1, SUB - 1))
        next_jump = jnp.where(window + 1 < SUB, next_jump, jnp.zeros_like(next_jump))
        misfit = obs_precision[window].astype(jnp.float32) * (end_state[window] - innovation[window].astype(jnp.float32))
        gradient = own_jump + adjoint(misfit - next_jump, diffusion[window].astype(jnp.float32),
                                      sub_steps[window], mode_in, mode_out)
        pert_here = lax.dynamic_index_in_dim(ens_pert, window, 1, keepdims=False)
        contrib = jnp.sum(pert_here.astype(jnp.float32) * gradient[None], axis=-1)
        summed = jax.ops.segment_sum(contrib.reshape(MEM, -1).T, segment_ids, num_segments=SLABS * CSLAB)
        return gradient, summed.T.reshape(MEM, SLABS, CSLAB)

    gradients, partial_terms = lax.map(gradient_of, windows)
    return gradients, ens_weight + jnp.sum(partial_terms, axis=0)
```

```python
import jax
import jax.numpy as jnp
from jax import lax
from jax.experimental import pallas as pl
from jax.experimental.pallas import tpu as pltpu
from jax.sharding import PartitionSpec as P

MESH = pl.DeviceIdType.MESH
F32, BF16 = jnp.float32, jnp.bfloat16
GROUP = 2
LAST = (((1,), (1,)), ((), ()))


def halves(x):
    high = x.astype(BF16)
    low = (x - high.astype(F32)).astype(BF16)
    return jnp.concatenate([high, low], axis=0)


def kernel(
    tm_count, lat_count, sizes,
    steps_ref, incr_h, pert_h, weight_h, cmap_h, diff_h, min_h, mout_h, prec_h, obs_h, innov_h,
    grad_h, gw_ref,
    incr, pert, gathered, cmap, cpad, diff, m_in, m_out, prec, obs, innov,
    onehot, start, start_bf, a_buf, b_buf, state_halo, start_next, prec_next,
    end_bf, end_prev, u_buf, seed_bf, seed_halo, c_buf, w_buf, mw_t, contrib,
    term_send, term_recv, local_sem, send_sem, recv_sem, ag_send, ag_recv, rs_send, rs_recv,
):
    H, R, LON, LEV, MEM, CW = sizes
    C = CW * tm_count
    PAD = cpad.shape[1]
    me_t, me_l = lax.axis_index("tm"), lax.axis_index("lat")
    has_up, has_down = me_l > 0, me_l < lat_count - 1
    has_prev, has_next = me_t > 0, me_t < tm_count - 1

    def local(i, src, dst):
        return pltpu.make_async_copy(src, dst, local_sem.at[i])

    def remote(i, src, dst, tm, lat):
        return pltpu.make_async_remote_copy(
            src_ref=src, dst_ref=dst, send_sem=send_sem.at[i], recv_sem=recv_sem.at[i],
            device_id=(tm, lat), device_id_type=MESH,
        )

    loads = dict(
        weight=local(0, weight_h.at[:, 0], gathered.at[me_t]),
        cmap=local(1, cmap_h, cmap),
        pert=local(2, pert_h.at[:, 0], pert),
        incr=local(3, incr_h.at[0], incr),
        diff=local(4, diff_h.at[0], diff.at[pl.ds(H, R)]),
        m_in=local(5, min_h, m_in),
        m_out=local(6, mout_h, m_out),
        prec=local(7, prec_h.at[0], prec),
        obs=local(8, obs_h.at[0], obs),
        innov=local(9, innov_h.at[0], innov),
    )
    for copy in loads.values():
        copy.start()

    barrier = pltpu.get_barrier_semaphore()
    for d in range(1, tm_count):
        pl.semaphore_signal(barrier, inc=1, device_id=(lax.rem(me_t + d, tm_count), me_l), device_id_type=MESH)

    @pl.when(has_up)
    def _():
        pl.semaphore_signal(barrier, inc=1, device_id=(me_t, me_l - 1), device_id_type=MESH)

    @pl.when(has_down)
    def _():
        pl.semaphore_signal(barrier, inc=1, device_id=(me_t, me_l + 1), device_id_type=MESH)

    @pl.when(jnp.logical_not(has_up))
    def _():
        diff[0:H] = jnp.zeros((H, LON, LEV), BF16)
        state_halo[0] = jnp.zeros((H, LON, LEV), BF16)
        seed_halo[0] = jnp.zeros((H, LON, LEV), BF16)

    @pl.when(jnp.logical_not(has_down))
    def _():
        diff[H + R:2 * H + R] = jnp.zeros((H, LON, LEV), BF16)
        state_halo[1] = jnp.zeros((H, LON, LEV), BF16)
        seed_halo[1] = jnp.zeros((H, LON, LEV), BF16)

    @pl.when(jnp.logical_not(has_prev))
    def _():
        end_prev[...] = jnp.zeros((R, LON, LEV), BF16)

    @pl.when(jnp.logical_not(has_next))
    def _():
        start_next[...] = jnp.zeros((R, LON, LEV), BF16)
        prec_next[...] = jnp.zeros((R, LON, LEV), BF16)

    loads["weight"].wait()
    pl.semaphore_wait(barrier, tm_count - 1 + has_up.astype(jnp.int32) + has_down.astype(jnp.int32))

    def spread(d):
        peer = lax.rem(me_t + d, tm_count)
        return pltpu.make_async_remote_copy(
            src_ref=gathered.at[me_t], dst_ref=gathered.at[me_t], send_sem=ag_send.at[d],
            recv_sem=ag_recv.at[d], device_id=(peer, me_l), device_id_type=MESH,
        )

    def term(d):
        peer = lax.rem(me_t + d, tm_count)
        return pltpu.make_async_remote_copy(
            src_ref=term_send.at[peer], dst_ref=term_recv.at[me_t], send_sem=rs_send.at[d],
            recv_sem=rs_recv.at[d], device_id=(peer, me_l), device_id_type=MESH,
        )

    for d in range(1, tm_count):
        spread(d).start()

    diff_up = remote(0, diff_h.at[0, pl.ds(0, H)], diff.at[pl.ds(H + R, H)], me_t, me_l - 1)
    diff_down = remote(1, diff_h.at[0, pl.ds(R - H, H)], diff.at[pl.ds(0, H)], me_t, me_l + 1)
    prec_back = remote(2, prec_h.at[0], prec_next, me_t - 1, me_l)
    start_back = remote(3, start_bf, start_next, me_t - 1, me_l)
    end_on = remote(4, end_bf, end_prev, me_t + 1, me_l)
    Q = GROUP if H % GROUP == 0 else 1
    parts = H // Q

    def edge_copies(base, field, halo):
        ups, downs = [], []
        for c in range(parts):
            first = c * Q
            ups.append(remote(base + c, field.at[pl.ds(first, Q)], halo.at[1, pl.ds(first, Q)], me_t, me_l - 1))
            first = H - (c + 1) * Q
            downs.append(remote(
                base + parts + c, field.at[pl.ds(R - H + first, Q)], halo.at[0, pl.ds(first, Q)], me_t, me_l + 1
            ))
        return ups, downs

    state_up, state_down = edge_copies(5, start_bf, state_halo)
    seed_up, seed_down = edge_copies(5 + 2 * parts, seed_bf, seed_halo)

    def go(copy, there):
        @pl.when(there)
        def _():
            copy.start()

    def sent(copy, there):
        @pl.when(there)
        def _():
            copy.wait_send()

    def got(copy, there):
        @pl.when(there)
        def _():
            copy.wait_recv()

    go(diff_up, has_up)
    go(diff_down, has_down)
    go(prec_back, has_prev)

    loads["cmap"].wait()
    cpad[...] = jnp.full(cpad.shape, -1, jnp.int32)
    cpad[:, 0:LON] = cmap[...]
    contrib[...] = jnp.zeros(contrib.shape, F32)
    LANES = PAD
    CH = 128 if C % 128 == 0 else C

    def indicate(chunk, carry):
        base = pl.multiple_of(chunk * CH, CH)
        rows = lax.broadcasted_iota(jnp.int32, (CH, LANES), 0) + base
        for i in range(R):
            hit = jnp.where(rows == cpad[i:i + 1, :], 1.0, 0.0).astype(BF16)
            onehot[pl.ds(base, CH), i * LANES:(i + 1) * LANES] = hit
        return carry

    lax.fori_loop(0, C // CH, indicate, 0)

    for d in range(1, tm_count):
        spread(d).wait_recv()
    weights = jnp.concatenate([gathered[p] for p in range(tm_count)], axis=1)
    picked = jnp.dot(halves(weights), onehot[...], preferred_element_type=F32)
    mw_t[...] = jnp.transpose(picked[0:MEM] + picked[MEM:2 * MEM])

    loads["pert"].wait()
    loads["incr"].wait()

    def begin(first, count):
        for i in range(first, first + count):
            cols = mw_t[i * LANES:i * LANES + LON, :]
            row = incr[i]
            for k in range(MEM):
                row = row + pert[k, i].astype(F32) * cols[:, k:k + 1]
            start[i] = row
            a_buf[i + H] = row
            start_bf[i] = row.astype(BF16)

    def blocks(row, first, count):
        done = 0
        while done < count:
            size = min(GROUP, count - done)
            row(first + done, size)
            done += size

    def from_edges(row, ups, downs):
        for c in range(parts):
            row(c * Q, Q)
            go(ups[c], has_up)
            row(R - (c + 1) * Q, Q)
            go(downs[c], has_down)
        blocks(row, H, R - 2 * H)

    from_edges(begin, state_up, state_down)
    go(start_back, has_prev)

    step_count = steps_ref[0]
    loads["diff"].wait()
    loads["m_in"].wait()
    loads["m_out"].wait()

    def laplacian(field, r, count):
        here = field[pl.ds(r, count)]
        sides = pltpu.roll(here, 1, 1) + pltpu.roll(here, LON - 1, 1)
        return here, field[pl.ds(r - 1, count)] + field[pl.ds(r + 1, count)] + sides - 4.0 * here

    def forward_rows(n, src, dst, r, count):
        here, lap = laplacian(src, r, count)
        smoothed = here + diff[pl.ds(r, count)].astype(F32) * lap
        flat = smoothed.astype(BF16).reshape(count * LON, LEV)
        modes = jnp.dot(flat, m_in[n], preferred_element_type=F32).astype(BF16)
        moved = jnp.dot(modes, m_out[n], preferred_element_type=F32)
        advanced = smoothed + moved.reshape(count, LON, LEV)
        result = jnp.where(n < step_count, advanced, here)
        dst[pl.ds(r, count)] = result
        return result

    def buffers(n):
        return (a_buf, b_buf) if n % 2 == 0 else (b_buf, a_buf)

    def forward_inner(n):
        src, dst = buffers(n)
        blocks(lambda r, c: forward_rows(n, src, dst, r, c), H + n + 1, R - 2 * n - 2)

    def forward_edges(n):
        src, dst = buffers(n)
        blocks(lambda r, c: forward_rows(n, src, dst, r, c), n + 1, H)
        blocks(lambda r, c: forward_rows(n, src, dst, r, c), H + R - n - 1, H)

    for n in range(H - 1):
        forward_inner(n)
    got(diff_up, has_down)
    got(diff_down, has_up)
    for copy in state_up:
        got(copy, has_down)
    for copy in state_down:
        got(copy, has_up)

    def widen(i, carry):
        a_buf[i] = state_halo[0, i].astype(F32)
        a_buf[i + H + R] = state_halo[1, i].astype(F32)
        return carry

    lax.fori_loop(0, H, widen, 0)
    for n in range(H - 1):
        forward_edges(n)
    loads["obs"].wait()
    loads["innov"].wait()
    got(prec_back, has_next)
    got(start_back, has_next)
    src, dst = buffers(H - 1)

    def finish(i, count):
        rows = pl.ds(i, count)
        end = forward_rows(H - 1, src, dst, i + H, count)
        misfit = obs[rows].astype(F32) * (end - innov[rows].astype(F32))
        seed = misfit - prec_next[rows].astype(F32) * (start_next[rows].astype(F32) - end)
        end_bf[rows] = end.astype(BF16)
        u_buf[pl.ds(i + H, count)] = seed
        seed_bf[rows] = seed.astype(BF16)

    from_edges(finish, seed_up, seed_down)
    go(end_on, has_next)

    def couple(m, r, count):
        n = H - 1 - m
        rows = pl.ds(r, count)
        here = u_buf[rows]
        flat = here.astype(BF16).reshape(count * LON, LEV)
        modes = lax.dot_general(flat, m_out[n], LAST, preferred_element_type=F32).astype(BF16)
        moved = lax.dot_general(modes, m_in[n], LAST, preferred_element_type=F32)
        coupled = here + moved.reshape(count, LON, LEV)
        c_buf[m % 2, rows] = coupled
        w_buf[m % 2, rows] = diff[rows].astype(F32) * coupled

    def settle(m, r, count):
        rows = pl.ds(r, count)
        _, lap = laplacian(w_buf.at[m % 2], r, count)
        u_buf[rows] = jnp.where(H - 1 - m < step_count, c_buf[m % 2, rows] + lap, u_buf[rows])

    for m in range(H):
        blocks(lambda r, c: couple(m, r, c), H + m, R - 2 * m)
        blocks(lambda r, c: settle(m, r, c), H + m + 1, R - 2 * m - 2)
    for copy in seed_up:
        got(copy, has_down)
    for copy in seed_down:
        got(copy, has_up)

    def widen_seed(i, carry):
        u_buf[i] = seed_halo[0, i].astype(F32)
        u_buf[i + H + R] = seed_halo[1, i].astype(F32)
        return carry

    lax.fori_loop(0, H, widen_seed, 0)
    for m in range(H):
        blocks(lambda r, c: couple(m, r, c), m, H)
        blocks(lambda r, c: couple(m, r, c), H + R - m, H)
        blocks(lambda r, c: settle(m, r, c), m + 1, H)
        blocks(lambda r, c: settle(m, r, c), H + R - m - 1, H)

    got(end_on, has_prev)
    loads["prec"].wait()
    lane = lax.broadcasted_iota(jnp.int32, (MEM, MEM * LEV), 1)
    member = lax.broadcasted_iota(jnp.int32, (MEM, MEM * LEV), 0) * LEV
    own = jnp.where((lane >= member) & (lane < member + LEV), 1.0, 0.0).astype(BF16)

    for i in range(R):
        jump = prec[i].astype(F32) * (start[i] - end_prev[i].astype(F32))
        total = jump + u_buf[i + H]
        grad_h[0, i] = total
        terms = jnp.concatenate([(pert[k, i].astype(F32) * total).astype(BF16) for k in range(MEM)], axis=1)
        contrib[:, i * LANES:i * LANES + LON] = lax.dot_general(own, terms, LAST, preferred_element_type=F32)

    sums = lax.dot_general(halves(contrib[...]), onehot[...], LAST, preferred_element_type=F32)
    sums = sums[0:MEM] + sums[MEM:2 * MEM]
    for p in range(tm_count):
        term_send[p] = sums[:, p * CW:(p + 1) * CW]
    for d in range(1, tm_count):
        term(d).start()
    result = gathered[me_t] + term_send[me_t]
    for d in range(1, tm_count):
        term(d).wait_recv()
    for d in range(1, tm_count):
        result = result + term_recv[lax.rem(me_t + d, tm_count)]
    gw_ref[:, 0, :] = result

    for d in range(1, tm_count):
        spread(d).wait_send()
        term(d).wait_send()
    for copy in [diff_up] + state_up + seed_up:
        sent(copy, has_up)
    for copy in [diff_down] + state_down + seed_down:
        sent(copy, has_down)
    sent(prec_back, has_prev)
    sent(start_back, has_prev)
    sent(end_on, has_next)


def deliver(grad, owned, grad_h, gw_h, sem):
    copies = [
        pltpu.make_async_copy(grad, grad_h, sem.at[0]),
        pltpu.make_async_copy(owned, gw_h, sem.at[1]),
    ]
    for copy in copies:
        copy.start()
    for copy in copies:
        copy.wait()


def solution(mesh):
    tm_count, lat_count = mesh.shape["tm"], mesh.shape["lat"]

    def body(incr, pert, weight, cmap, steps, diffusion, m_in, m_out, prec, obs, innov):
        _, R, LON, LEV = incr.shape
        MEM, _, CW = weight.shape
        H = m_in.shape[0]
        PAD = -(-LON // 128) * 128
        field = lambda rows, kind: pltpu.VMEM((rows, LON, LEV), kind)
        wide = 2 * H + R
        scratch = [
            field(R, F32),
            pltpu.VMEM((MEM, R, LON, LEV), BF16),
            pltpu.VMEM((tm_count, MEM, CW), F32),
            pltpu.VMEM((R, LON), jnp.int32),
            pltpu.VMEM((R, PAD), jnp.int32),
            field(wide, BF16),
            pltpu.VMEM(m_in.shape, BF16),
            pltpu.VMEM(m_out.shape, BF16),
            field(R, BF16), field(R, BF16), field(R, BF16),
            pltpu.VMEM((CW * tm_count, R * PAD), BF16),
            field(R, F32), field(R, BF16), field(wide, F32), field(wide, F32),
            pltpu.VMEM((2, H, LON, LEV), BF16),
            field(R, BF16), field(R, BF16), field(R, BF16), field(R, BF16),
            field(wide, F32), field(R, BF16),
            pltpu.VMEM((2, H, LON, LEV), BF16),
            pltpu.VMEM((2, wide, LON, LEV), F32),
            pltpu.VMEM((2, wide, LON, LEV), F32),
            pltpu.VMEM((R * PAD, MEM), F32),
            pltpu.VMEM((MEM, R * PAD), F32),
            pltpu.VMEM((tm_count, MEM, CW), F32),
            pltpu.VMEM((tm_count, MEM, CW), F32),
            pltpu.SemaphoreType.DMA((11,)),
            pltpu.SemaphoreType.DMA((5 + 4 * H,)),
            pltpu.SemaphoreType.DMA((5 + 4 * H,)),
        ] + [pltpu.SemaphoreType.DMA((tm_count,))] * 4

        def run(*refs):
            kernel(tm_count, lat_count, (H, R, LON, LEV, MEM, CW), *refs)

        fixed = [
            pltpu.with_memory_space_constraint(x, pltpu.HBM)
            for x in (incr, pert, weight, cmap, diffusion, m_in, m_out, prec, obs, innov)
        ]
        grad, owned = pl.pallas_call(
            run,
            out_shape=(
                pltpu.VMEM(incr.shape, F32),
                pltpu.VMEM((MEM, 1, CW), F32),
            ),
            in_specs=[pl.BlockSpec(memory_space=pltpu.SMEM)] + [pl.BlockSpec(memory_space=pltpu.HBM)] * 10,
            out_specs=(pl.BlockSpec(memory_space=pltpu.VMEM), pl.BlockSpec(memory_space=pltpu.VMEM)),
            scratch_shapes=scratch,
            compiler_params=pltpu.CompilerParams(
                collective_id=0, has_side_effects=True, vmem_limit_bytes=48 * 1024 * 1024
            ),
        )(steps, *fixed)
        grad = pltpu.with_memory_space_constraint(grad, pltpu.VMEM)
        owned = pltpu.with_memory_space_constraint(owned, pltpu.VMEM)
        return pl.pallas_call(
            deliver,
            out_shape=(
                jax.ShapeDtypeStruct(incr.shape, F32),
                jax.ShapeDtypeStruct((MEM, 1, CW), F32),
            ),
            in_specs=[pl.BlockSpec(memory_space=pltpu.VMEM)] * 2,
            out_specs=(pl.BlockSpec(memory_space=pl.ANY), pl.BlockSpec(memory_space=pl.ANY)),
            scratch_shapes=[pltpu.SemaphoreType.DMA((2,))],
        )(grad, owned)
    return jax.shard_map(
        body,
        mesh=mesh,
        in_specs=(
            P("tm", "lat", None, None),
            P(None, "tm", "lat", None, None),
            P(None, "lat", "tm"),
            P("lat", None),
            P("tm"),
            P("tm", "lat", None, None),
            P(),
            P(),
            P("tm", "lat", None, None),
            P("tm", "lat", None, None),
            P("tm", "lat", None, None),
        ),
        out_specs=(P("tm", "lat", None, None), P(None, "lat", "tm")),
        check_vma=False,
    )
```

```python
import jax
import jax.numpy as jnp
from jax import lax
from jax.experimental import pallas as pl
from jax.experimental.pallas import tpu as pltpu
from jax.sharding import PartitionSpec as P

MESH = pl.DeviceIdType.MESH
F32, BF16 = jnp.float32, jnp.bfloat16
EDGE = 8
LANES = 128
WIDTH = 256


def supplied(k):
    return k // 2, k // 2 + k % 2 + 1


def kernel(
    tm_count, lat_count, sizes,
    steps_ref, incr_h, pert_h, weight_h, cmap_h, diff_h, min_h, mout_h, prec_h, obs_h, innov_h,
    grad_ref, gw_ref,
    incr, pert, gathered, cmap, diff, diff_halo, d_buf, e_buf, m_in, m_out, prec, obs, innov,
    both, both_t, cflat, sums_buf, onehot, start, start_bf, s_buf, w_buf, u_buf, ec_buf, end_buf, end_bf, end_prev, start_next, prec_next,
    fwd_send, fwd_recv, adj_send, adj_recv, contrib,
    term_send, term_recv, local_sem, send_sem, recv_sem, ag_send, ag_recv, rs_send, rs_recv,
):
    H, R, LON, LEV, MEM, CW = sizes
    C = CW * tm_count
    D = diff_halo.shape[1]
    DS = (s_buf.shape[1] - R) // 2
    HALF = R // 2
    GJ = WIDTH // MEM
    me_t, me_l = lax.axis_index("tm"), lax.axis_index("lat")
    has_up, has_down = me_l > 0, me_l < lat_count - 1
    has_prev, has_next = me_t > 0, me_t < tm_count - 1

    def pair(r):
        return (r, R - 1 - r)

    def local(i, src, dst):
        return pltpu.make_async_copy(src, dst, local_sem.at[i])

    count = [0]

    def remote(src, dst, tm, lat):
        i = count[0]
        count[0] += 1
        return pltpu.make_async_remote_copy(
            src_ref=src, dst_ref=dst, send_sem=send_sem.at[i], recv_sem=recv_sem.at[i],
            device_id=(tm, lat), device_id_type=MESH,
        )

    loads = dict(
        weight=local(0, weight_h.at[:, 0], gathered.at[me_t]),
        cmap=local(1, cmap_h, cmap),
        diff=local(2, diff_h.at[0], diff),
        pert=local(3, pert_h.at[:, 0], pert),
        incr=local(4, incr_h.at[0], incr),
        m_in=local(5, min_h, m_in),
        m_out=local(6, mout_h, m_out),
        obs=local(7, obs_h.at[0], obs),
        innov=local(8, innov_h.at[0], innov),
        prec=local(9, prec_h.at[0], prec),
    )
    barrier = pltpu.get_barrier_semaphore()
    for d in range(1, tm_count):
        pl.semaphore_signal(barrier, inc=1, device_id=(lax.rem(me_t + d, tm_count), me_l), device_id_type=MESH)

    @pl.when(has_up)
    def _():
        pl.semaphore_signal(barrier, inc=1, device_id=(me_t, me_l - 1), device_id_type=MESH)

    @pl.when(has_down)
    def _():
        pl.semaphore_signal(barrier, inc=1, device_id=(me_t, me_l + 1), device_id_type=MESH)

    for copy in loads.values():
        copy.start()

    def clear(side):
        diff_halo[side] = jnp.zeros((D, LON, LEV), BF16)
        fwd_recv[side] = jnp.zeros((H, LON, LEV), BF16)
        adj_recv[side] = jnp.zeros((H, LON, LEV), BF16)

    @pl.when(jnp.logical_not(has_up))
    def _():
        clear(0)

    @pl.when(jnp.logical_not(has_down))
    def _():
        clear(1)

    @pl.when(jnp.logical_not(has_prev))
    def _():
        end_prev[...] = jnp.zeros((R, LON, LEV), BF16)

    @pl.when(jnp.logical_not(has_next))
    def _():
        start_next[...] = jnp.zeros((R, LON, LEV), BF16)
        prec_next[...] = jnp.zeros((R, LON, LEV), BF16)

    loads["weight"].wait()
    pl.semaphore_wait(barrier, tm_count - 1 + has_up.astype(jnp.int32) + has_down.astype(jnp.int32))

    def spread(d):
        peer = lax.rem(me_t + d, tm_count)
        return pltpu.make_async_remote_copy(
            src_ref=gathered.at[me_t], dst_ref=gathered.at[me_t], send_sem=ag_send.at[d],
            recv_sem=ag_recv.at[d], device_id=(peer, me_l), device_id_type=MESH,
        )

    def term(d):
        peer = lax.rem(me_t + d, tm_count)
        return pltpu.make_async_remote_copy(
            src_ref=term_send.at[peer], dst_ref=term_recv.at[me_t], send_sem=rs_send.at[d],
            recv_sem=rs_recv.at[d], device_id=(peer, me_l), device_id_type=MESH,
        )

    for d in range(1, tm_count):
        spread(d).start()

    diff_up = remote(diff_h.at[0, pl.ds(0, D)], diff_halo.at[1], me_t, me_l - 1)
    diff_down = remote(diff_h.at[0, pl.ds(R - D, D)], diff_halo.at[0], me_t, me_l + 1)
    prec_back = [remote(prec_h.at[0, i], prec_next.at[i], me_t - 1, me_l) for i in range(R)]
    start_back = [remote(start_bf.at[i], start_next.at[i], me_t - 1, me_l) for i in range(R)]
    end_on = [remote(end_bf.at[i], end_prev.at[i], me_t + 1, me_l) for i in range(R)]
    fwd_up, fwd_down, adj_up, adj_down = [], [], [], []
    for k in range(H):
        n, depth = supplied(k)
        first, last = depth - 1, R - depth
        up_src = start_bf.at[first] if n == 0 else fwd_send.at[0, k]
        down_src = start_bf.at[last] if n == 0 else fwd_send.at[1, k]
        fwd_up.append(remote(up_src, fwd_recv.at[1, k], me_t, me_l - 1))
        fwd_down.append(remote(down_src, fwd_recv.at[0, k], me_t, me_l + 1))
        adj_up.append(remote(adj_send.at[0, k], adj_recv.at[1, k], me_t, me_l - 1))
        adj_down.append(remote(adj_send.at[1, k], adj_recv.at[0, k], me_t, me_l + 1))

    def go(there, *copies):
        @pl.when(there)
        def _():
            for copy in copies:
                copy.start()

    def sent(there, *copies):
        @pl.when(there)
        def _():
            for copy in copies:
                copy.wait_send()

    def got(there, *copies):
        @pl.when(there)
        def _():
            for copy in copies:
                copy.wait_recv()

    def rows_of(copies, r):
        return [copies[i] for i in pair(r)]

    go(has_up, diff_up)
    go(has_down, diff_down)
    early = [r for r in (1, 0, 2) if r < HALF]
    late = [r for r in range(HALF) if r not in early]
    for r in early:
        go(has_prev, *rows_of(prec_back, r))

    loads["cmap"].wait()
    for r in range(HALF):
        for s, i in enumerate(pair(r)):
            at = (2 * r + s) * LON
            cflat[:, at:at + LON] = cmap[i:i + 1, :]
    for c in range(0, C, LANES):
        rows = lax.broadcasted_iota(jnp.int32, (LANES, R * LON), 0) + c
        onehot[c:c + LANES, :] = jnp.where(rows == cflat[...], 1.0, 0.0).astype(BF16)
    loads["diff"].wait()

    def widen_diff(value, i):
        wide = value.astype(F32)
        d_buf[i] = wide
        e_buf[i] = 1.0 - 4.0 * wide

    for i in range(R):
        widen_diff(diff[i], i + D)
    loads["pert"].wait()
    loads["incr"].wait()
    loads["m_in"].wait()
    loads["m_out"].wait()
    for n in range(H):
        product = jnp.dot(m_in[n], m_out[n], preferred_element_type=F32)
        both[n] = product.astype(BF16)
        both_t[n] = jnp.transpose(product).astype(BF16)
    loads["obs"].wait()
    loads["innov"].wait()
    loads["prec"].wait()
    step_count = steps_ref[0]

    def put(buf, n, i, value):
        buf[n, i, EDGE:EDGE + LON] = value
        buf[n, i, EDGE - 1:EDGE] = value[LON - 1:LON]
        buf[n, i, EDGE + LON:EDGE + LON + 1] = value[0:1]

    def around(buf, n, i):
        north, south = buf[n, i - 1, EDGE:EDGE + LON], buf[n, i + 1, EDGE:EDGE + LON]
        west, east = buf[n, i, EDGE - 1:EDGE - 1 + LON], buf[n, i, EDGE + 1:EDGE + 1 + LON]
        return (north + south) + (west + east)

    def fwd_row(n, r, value, send=True):
        for s, i in enumerate(pair(r)):
            put(s_buf, n, i + DS, value[s])
        for k in range(H):
            if send and supplied(k) == (n, r + 1):
                if n > 0:
                    for s in range(2):
                        fwd_send[s, k] = value[s].astype(BF16)
                go(has_up, fwd_up[k])
                go(has_down, fwd_down[k])

    row = lax.broadcasted_iota(jnp.int32, (GJ, WIDTH), 0)
    lane = lax.broadcasted_iota(jnp.int32, (GJ, WIDTH), 1)
    own_cell = lax.rem(lane, GJ) == row
    groups = LON // GJ

    def places(r):
        found = []
        for at in range(2 * r * LON, 2 * (r + 1) * LON, LANES):
            index = jnp.broadcast_to(cflat[:, at:at + LANES], (MEM, LANES))
            found.append((index // LANES, index % LANES))
        return found

    placed = [places(r) for r in range(HALF)]
    repeat_row = lax.broadcasted_iota(jnp.int32, (MEM, WIDTH), 0)
    repeat_lane = lax.broadcasted_iota(jnp.int32, (MEM, WIDTH), 1) // GJ
    repeat = jnp.where(repeat_row == repeat_lane, 1.0, 0.0).astype(BF16)

    for d in range(1, tm_count):
        spread(d).wait_recv()
    weights = jnp.concatenate([gathered[p] for p in range(tm_count)], axis=1)
    def pick(r):
        found = []
        for block, inside in placed[r]:
            value = jnp.zeros((MEM, LANES), F32)
            for c in range(C // LANES):
                taken = jnp.take_along_axis(weights[:, c * LANES:(c + 1) * LANES], inside, axis=1)
                value = jnp.where(block == c, taken, value)
            found.append(jnp.transpose(value))
        return jnp.concatenate(found, axis=0).astype(BF16)

    def begin(r):
        cells = pick(r)
        picked = jnp.dot(cells, repeat, preferred_element_type=F32)
        value = []
        for s, i in enumerate(pair(r)):
            pieces = []
            for g in range(groups):
                at = g * GJ
                block = jnp.where(own_cell, picked[s * LON + at:s * LON + at + GJ], 0.0).astype(BF16)
                members = pert[:, i, at:at + GJ, :].reshape(WIDTH, LEV)
                pieces.append(incr[i, at:at + GJ] + jnp.dot(block, members, preferred_element_type=F32))
            state = jnp.concatenate(pieces, axis=0)
            start[i] = state
            start_bf[i] = state.astype(BF16)
            value.append(state)
        fwd_row(0, r, value)
        go(has_prev, *rows_of(start_back, r))

    def modes(value, both):
        flat = jnp.concatenate([v.astype(BF16) for v in value], axis=0)
        moved = jnp.dot(flat, both, preferred_element_type=F32)
        return [value[s] + moved[s * LON:(s + 1) * LON] for s in range(2)]

    def step(n, r):
        here = [s_buf[n, i + DS, EDGE:EDGE + LON] for i in pair(r)]
        smoothed = [e_buf[i + D] * here[s] + d_buf[i + D] * around(s_buf, n, i + DS) for s, i in enumerate(pair(r))]
        result = modes(smoothed, both[n])
        if n > 0:
            result = [jnp.where(n < step_count, a, b) for a, b in zip(result, here)]
        if n + 1 < H:
            fwd_row(n + 1, r, result)
        else:
            for s, i in enumerate(pair(r)):
                end_buf[i] = result[s]
                end_bf[i] = result[s].astype(BF16)
            go(has_next, *rows_of(end_on, r))

    def fold(r):
        return R - 1 - r if r >= HALF else r

    def needs_state(n, r, found):
        if (n, r) in found:
            return
        found.add((n, r))
        if n == 0 or (r < 0 and n <= -r - 1):
            return
        for near in (r - 1, r, r + 1):
            needs_state(n - 1, fold(near), found)

    wanted = set()
    for r in range(HALF):
        needs_state(H, r, wanted)
    known = set()

    def forward():
        while True:
            ready = [
                (n, r) for n, r in sorted(wanted) if (n, r) not in known and n > 0
                and not (r < 0 and n <= -r - 1)
                and all((n - 1, fold(q)) in known for q in (r - 1, r, r + 1))
            ]
            if not ready:
                return
            for n, r in ready:
                step(n - 1, r)
                known.add((n, r))

    for r in range(HALF):
        begin(r)
        known.add((0, r))
        if r == max(early):
            for q in late:
                go(has_prev, *rows_of(prec_back, q))
        forward()

    wanted_u, wanted_w = set(), set()

    def needs_u(m, r):
        if (m, r) in wanted_u:
            return
        wanted_u.add((m, r))
        if m == 0 or (r < 0 and m <= -r - 1):
            return
        needs_u(m - 1, r)
        for near in (r - 1, r, r + 1):
            needs_w(m - 1, fold(near))

    def needs_w(m, r):
        if (m, r) in wanted_w:
            return
        wanted_w.add((m, r))
        if not (r < 0 and m <= -r - 1):
            needs_u(m, r)

    for r in range(HALF):
        needs_u(H, r)
    known_u, known_w, coupled_at = set(), set(), set()

    def adj_send_row(k, value):
        for s in range(2):
            adj_send[s, k] = value[s].astype(BF16)
        go(has_up, adj_up[k])
        go(has_down, adj_down[k])

    def have_u(m, r, value):
        for s, i in enumerate(pair(r)):
            u_buf[i + D] = value[s]
        known_u.add((m, r))
        for k in range(0, H, 2):
            if r >= 0 and supplied(k) == (m, r + 1):
                adj_send_row(k, value)

    def couple(m, r):
        n = H - 1 - m
        here = [u_buf[i + D] for i in pair(r)]
        coupled = modes(here, both_t[n])
        weighted = [d_buf[i + D] * coupled[s] for s, i in enumerate(pair(r))]
        for s, i in enumerate(pair(r)):
            ec_buf[i + D] = e_buf[i + D] * coupled[s]
            put(w_buf, m, i + DS, weighted[s])
        for k in range(1, H, 2):
            if r >= 0 and supplied(k) == (m, r + 1):
                adj_send_row(k, weighted)

    def settle(m, r):
        value = []
        for s, i in enumerate(pair(r)):
            result = ec_buf[i + D] + around(w_buf, m, i + DS)
            if m < H - 1:
                result = jnp.where(H - 1 - m < step_count, result, u_buf[i + D])
            value.append(result)
        if m + 1 < H:
            have_u(m + 1, r, value)
        else:
            known_u.add((H, r))
            final(r, value)

    level_row = lax.broadcasted_iota(jnp.int32, (MEM * LEV, 2 * MEM), 0) // LEV
    level_lane = lax.broadcasted_iota(jnp.int32, (MEM * LEV, 2 * MEM), 1) % MEM
    own = jnp.where(level_row == level_lane, 1.0, 0.0).astype(BF16)
    is_high = lax.broadcasted_iota(jnp.int32, (2 * LON, 2 * MEM), 1) < MEM
    cut = max(HALF // 2, 1)
    parts = [list(range(0, cut)), list(range(cut, HALF))]
    totals = []

    def final(r, value):
        got(has_prev, *rows_of(end_on, r))
        terms = []
        for s, i in enumerate(pair(r)):
            total = prec[i].astype(F32) * (start[i] - end_prev[i].astype(F32)) + value[s]
            grad_ref[0, i] = total
            rounded = total.astype(BF16)
            terms.append(jnp.concatenate([pert[k, i] * rounded for k in range(MEM)], axis=1))
        summed = jnp.concatenate([jnp.dot(t, own, preferred_element_type=F32) for t in terms], axis=0)
        high = summed.astype(BF16).astype(F32)
        at = 2 * r * LON
        contrib[at:at + 2 * LON] = jnp.where(is_high, high, summed - high).astype(BF16)
        for part in parts:
            if r in part and all((H, q) in known_u for q in part):
                at, until = 2 * part[0] * LON, 2 * (part[-1] + 1) * LON
                share = jnp.dot(onehot[:, at:until], contrib[at:until], preferred_element_type=F32)
                if totals:
                    share = share + sums_buf[...]
                sums_buf[...] = share
                totals.append(part)

    def leading(goals):
        need_c, need_s, stack = set(), set(), []
        for m, r in goals:
            stack.append(("c" if (m, r + 1) in [supplied(k) for k in range(1, H, 2)] else "u", m, r))
        while stack:
            kind, m, r = stack.pop()
            if kind == "c" and (m, r) not in need_c:
                need_c.add((m, r))
                stack.append(("u", m, r))
            elif kind == "u" and m > 0 and (m - 1, r) not in need_s:
                need_s.add((m - 1, r))
                stack.extend(("c", m - 1, fold(q)) for q in (r - 1, r, r + 1))
        return need_c, need_s

    def adjoint(goals=None):
        only = leading(goals) if goals else None
        while True:
            ready = [("c", m, r) for m, r in sorted(known_u) if m < H and (m, r) not in coupled_at
                     and ((m, r) in wanted_w or (m + 1, r) in wanted_u)]
            ready += [
                ("s", m - 1, r) for m, r in sorted(wanted_u) if m > 0 and (m, r) not in known_u
                and not (r < 0 and m <= -r - 1) and (m - 1, r) in coupled_at
                and all((m - 1, fold(q)) in known_w for q in (r - 1, r, r + 1))
            ]
            if only:
                ready = [t for t in ready if t[1:] in only[0 if t[0] == "c" else 1]]
            if not ready:
                return
            for kind, m, r in ready:
                if kind == "c":
                    couple(m, r)
                    coupled_at.add((m, r))
                    known_w.add((m, r))
                else:
                    settle(m, r)

    def seed(r):
        value = []
        for i in pair(r):
            end = end_buf[i]
            misfit = obs[i].astype(F32) * (end - innov[i].astype(F32))
            value.append(misfit - prec_next[i].astype(F32) * (start_next[i].astype(F32) - end))
        have_u(0, r, value)

    got(has_down, diff_up)
    got(has_up, diff_down)
    for q in range(1, D + 1):
        widen_diff(diff_halo[0, D - q], D - q)
        widen_diff(diff_halo[1, q - 1], R - 1 + D + q)

    urgent = {(supplied(k)[0], supplied(k)[1] - 1) for k in range(H)}

    def seed_and_send(r):
        got(has_next, *rows_of(prec_back, r), *rows_of(start_back, r))
        seed(r)
        adjoint(urgent)

    split = max(H - 2, 0)
    seeded = []
    for some in [range(split)] + [range(k, k + 1) for k in range(split, H)]:
        for k in some:
            got(has_down, fwd_up[k])
            got(has_up, fwd_down[k])
        for k in some:
            n, depth = supplied(k)
            fwd_row(n, -depth, [fwd_recv[s, k].astype(F32) for s in range(2)], send=False)
            known.add((n, -depth))
        forward()
        if (H, 1) in known and not seeded:
            seed_and_send(1)
            seeded.append(1)
    for r in range(HALF):
        if r not in seeded:
            seed_and_send(r)
    adjoint()

    order = [1, 0] + list(range(2, H)) if H > 1 else [0]
    for first in range(0, H, 2):
        some = order[first:first + 2]
        for k in some:
            got(has_down, adj_up[k])
            got(has_up, adj_down[k])
        for k in some:
            m, depth = supplied(k)
            value = [adj_recv[s, k].astype(F32) for s in range(2)]
            if k % 2 == 0:
                have_u(m, -depth, value)
            else:
                for s, i in enumerate(pair(-depth)):
                    put(w_buf, m, i + DS, value[s])
                known_w.add((m, -depth))
        adjoint()

    sums = jnp.transpose(sums_buf[...])
    sums = sums[0:MEM] + sums[MEM:2 * MEM]
    for p in range(tm_count):
        term_send[p] = sums[:, p * CW:(p + 1) * CW]
    for d in range(1, tm_count):
        term(d).start()
    result = gathered[me_t] + term_send[me_t]
    for d in range(1, tm_count):
        term(d).wait_recv()
    for d in range(1, tm_count):
        result = result + term_recv[lax.rem(me_t + d, tm_count)]
    gw_ref[:, 0, :] = result

    for d in range(1, tm_count):
        spread(d).wait_send()
        term(d).wait_send()
    sent(has_up, diff_up, *fwd_up, *adj_up)
    sent(has_down, diff_down, *fwd_down, *adj_down)
    sent(has_prev, *prec_back, *start_back)
    sent(has_next, *end_on)


def deliver(grad, owned, grad_h, gw_h, sem):
    copies = [
        pltpu.make_async_copy(grad, grad_h, sem.at[0]),
        pltpu.make_async_copy(owned, gw_h, sem.at[1]),
    ]
    for copy in copies:
        copy.start()
    for copy in copies:
        copy.wait()


def solution(mesh):
    tm_count, lat_count = mesh.shape["tm"], mesh.shape["lat"]

    def body(incr, pert, weight, cmap, steps, diffusion, m_in, m_out, prec, obs, innov):
        _, R, LON, LEV = incr.shape
        MEM, _, CW = weight.shape
        H = m_in.shape[0]
        D = max(H // 2, 1)
        DS = max(supplied(k)[1] for k in range(H))
        C = CW * tm_count
        field = lambda rows, kind: pltpu.VMEM((rows, LON, LEV), kind)
        padded = pltpu.VMEM((H, R + 2 * DS, LON + 2 * EDGE, LEV), F32)
        halo = pltpu.VMEM((2, H, LON, LEV), BF16)
        scratch = [
            field(R, F32),
            pltpu.VMEM((MEM, R, LON, LEV), BF16),
            pltpu.VMEM((tm_count, MEM, CW), F32),
            pltpu.VMEM((R, LON), jnp.int32),
            field(R, BF16),
            pltpu.VMEM((2, D, LON, LEV), BF16),
            field(R + 2 * D, F32), field(R + 2 * D, F32),
            pltpu.VMEM(m_in.shape, BF16),
            pltpu.VMEM(m_out.shape, BF16),
            field(R, BF16), field(R, BF16), field(R, BF16),
            pltpu.VMEM((H, LEV, LEV), BF16),
            pltpu.VMEM((H, LEV, LEV), BF16),
            pltpu.VMEM((1, R * LON), jnp.int32),
            pltpu.VMEM((C, 2 * MEM), F32),
            pltpu.VMEM((C, R * LON), BF16),
            field(R, F32), field(R, BF16), padded, padded,
            field(R + 2 * D, F32), field(R + 2 * D, F32),
            field(R, F32), field(R, BF16), field(R, BF16), field(R, BF16), field(R, BF16),
            halo, halo, halo, halo,
            pltpu.VMEM((R * LON, 2 * MEM), BF16),
            pltpu.VMEM((tm_count, MEM, CW), F32),
            pltpu.VMEM((tm_count, MEM, CW), F32),
            pltpu.SemaphoreType.DMA((10,)),
            pltpu.SemaphoreType.DMA((2 + 3 * R + 4 * H,)),
            pltpu.SemaphoreType.DMA((2 + 3 * R + 4 * H,)),
        ] + [pltpu.SemaphoreType.DMA((tm_count,))] * 4

        def run(*refs):
            kernel(tm_count, lat_count, (H, R, LON, LEV, MEM, CW), *refs)

        fixed = [
            pltpu.with_memory_space_constraint(x, pltpu.HBM)
            for x in (incr, pert, weight, cmap, diffusion, m_in, m_out, prec, obs, innov)
        ]
        grad, owned = pl.pallas_call(
            run,
            out_shape=(
                pltpu.VMEM(incr.shape, F32),
                pltpu.VMEM((MEM, 1, CW), F32),
            ),
            in_specs=[pl.BlockSpec(memory_space=pltpu.SMEM)] + [pl.BlockSpec(memory_space=pltpu.HBM)] * 10,
            out_specs=(pl.BlockSpec(memory_space=pltpu.VMEM), pl.BlockSpec(memory_space=pltpu.VMEM)),
            scratch_shapes=scratch,
            compiler_params=pltpu.CompilerParams(
                collective_id=0, has_side_effects=True, vmem_limit_bytes=48 * 1024 * 1024
            ),
        )(steps, *fixed)
        grad = pltpu.with_memory_space_constraint(grad, pltpu.VMEM)
        owned = pltpu.with_memory_space_constraint(owned, pltpu.VMEM)
        return pl.pallas_call(
            deliver,
            out_shape=(
                jax.ShapeDtypeStruct(incr.shape, F32),
                jax.ShapeDtypeStruct((MEM, 1, CW), F32),
            ),
            in_specs=[pl.BlockSpec(memory_space=pltpu.VMEM)] * 2,
            out_specs=(pl.BlockSpec(memory_space=pl.ANY), pl.BlockSpec(memory_space=pl.ANY)),
            scratch_shapes=[pltpu.SemaphoreType.DMA((2,))],
        )(grad, owned)

    return jax.shard_map(
        body,
        mesh=mesh,
        in_specs=(
            P("tm", "lat", None, None),
            P(None, "tm", "lat", None, None),
            P(None, "lat", "tm"),
            P("lat", None),
            P("tm"),
            P("tm", "lat", None, None),
            P(),
            P(),
            P("tm", "lat", None, None),
            P("tm", "lat", None, None),
            P("tm", "lat", None, None),
        ),
        out_specs=(P("tm", "lat", None, None), P(None, "lat", "tm")),
        check_vma=False,
    )
```

```python
import jax
import jax.numpy as jnp
from jax import lax
from jax.experimental import pallas as pl
from jax.experimental.pallas import tpu as pltpu
from jax.sharding import PartitionSpec as P

MESH = pl.DeviceIdType.MESH
F32, BF16 = jnp.float32, jnp.bfloat16
EDGE = 8
LANES = 128
WIDTH = 256


def supplied(k):
    return k // 2, k // 2 + k % 2 + 1


def kernel(
    tm_count, lat_count, sizes,
    steps_ref, incr_h, pert_h, weight_h, cmap_h, diff_h, min_h, mout_h, prec_h, obs_h, innov_h,
    grad_ref, gw_ref,
    incr, pert, gathered, cmap, diff, diff_halo, d_buf, e_buf, m_in, m_out, prec, obs, innov,
    both, both_t, cflat, sums_buf, in_group, in_lane, start, start_bf, s_buf, w_buf, u_buf, ec_buf, end_buf, end_bf, end_prev, start_next, prec_next,
    fwd_send, fwd_recv, adj_send, adj_recv,
    term_send, term_recv, local_sem, send_sem, recv_sem,
):
    H, R, LON, LEV, MEM, CW = sizes
    C = CW * tm_count
    D = diff_halo.shape[1]
    DS = (s_buf.shape[1] - R) // 2
    HALF = R // 2
    GJ = WIDTH // MEM
    GL, HB = min(GJ, CW), CW // min(GJ, CW)
    me_t, me_l = lax.axis_index("tm"), lax.axis_index("lat")
    has_up, has_down = me_l > 0, me_l < lat_count - 1
    has_prev, has_next = me_t > 0, me_t < tm_count - 1

    def pair(r):
        return (r, R - 1 - r)

    def local(i, src, dst):
        return pltpu.make_async_copy(src, dst, local_sem.at[i])

    def remote(src, dst, tm, lat, out, into):
        return pltpu.make_async_remote_copy(
            src_ref=src, dst_ref=dst, send_sem=send_sem.at[out], recv_sem=recv_sem.at[into],
            device_id=(tm, lat), device_id_type=MESH,
        )

    def all_sent(out, ref):
        remote(ref, ref, me_t, me_l, out, 0).wait_send()

    def all_here(into, ref):
        remote(ref, ref, me_t, me_l, 0, into).wait_recv()

    loads = dict(
        weight=local(0, weight_h.at[:, 0], gathered.at[me_t]),
        cmap=local(1, cmap_h, cmap),
        diff=local(2, diff_h.at[0], diff),
        pert=local(3, pert_h.at[:, 0], pert),
        incr=local(4, incr_h.at[0], incr),
        m_in=local(5, min_h, m_in),
        m_out=local(6, mout_h, m_out),
        obs=local(7, obs_h.at[0], obs),
        innov=local(8, innov_h.at[0], innov),
        prec=local(9, prec_h.at[0], prec),
    )
    barrier = pltpu.get_barrier_semaphore()
    for d in range(1, tm_count):
        pl.semaphore_signal(barrier, inc=1, device_id=(lax.rem(me_t + d, tm_count), me_l), device_id_type=MESH)

    @pl.when(has_up)
    def _():
        pl.semaphore_signal(barrier, inc=1, device_id=(me_t, me_l - 1), device_id_type=MESH)

    @pl.when(has_down)
    def _():
        pl.semaphore_signal(barrier, inc=1, device_id=(me_t, me_l + 1), device_id_type=MESH)

    for copy in loads.values():
        copy.start()

    def clear(side):
        diff_halo[side] = jnp.zeros((D, LON, LEV), BF16)
        fwd_recv[side] = jnp.zeros((H, LON, LEV), BF16)
        adj_recv[side] = jnp.zeros((H, LON, LEV), BF16)

    @pl.when(jnp.logical_not(has_up))
    def _():
        clear(0)

    @pl.when(jnp.logical_not(has_down))
    def _():
        clear(1)

    @pl.when(jnp.logical_not(has_prev))
    def _():
        end_prev[...] = jnp.zeros((R, LON, LEV), BF16)

    @pl.when(jnp.logical_not(has_next))
    def _():
        start_next[...] = jnp.zeros((R, LON, LEV), BF16)
        prec_next[...] = jnp.zeros((R, LON, LEV), BF16)

    loads["weight"].wait()
    pl.semaphore_wait(barrier, tm_count - 1 + has_up.astype(jnp.int32) + has_down.astype(jnp.int32))

    others = pl.ds(0, tm_count - 1)

    def spread(d):
        peer = lax.rem(me_t + d, tm_count)
        return remote(gathered.at[me_t], gathered.at[me_t], peer, me_l, 0, 0)

    def term(d):
        peer = lax.rem(me_t + d, tm_count)
        return remote(term_send.at[peer], term_recv.at[me_t], peer, me_l, 1, 1)

    for d in range(1, tm_count):
        spread(d).start()

    early_groups = [list(range(max(H - 2, 0)))] + [[k] for k in range(max(H - 2, 0), H)]
    adj_order = [1, 0] + list(range(2, H)) if H > 1 else [0]
    late_groups = [adj_order[k:k + 2] for k in range(0, H, 2)]
    early_groups = [g for g in early_groups if g]
    fwd_sem = {k: 4 + 2 * g for g, group in enumerate(early_groups) for k in group}
    adj_base = 4 + 2 * len(early_groups)
    adj_sem = {k: adj_base + 2 * g for g, group in enumerate(late_groups) for k in group}
    next_base = adj_base + 2 * len(late_groups)
    prev_base = next_base + HALF

    def pair_of(i):
        return min(i, R - 1 - i)

    diff_up = remote(diff_h.at[0, pl.ds(0, D)], diff_halo.at[1], me_t, me_l - 1, 2, 2)
    diff_down = remote(diff_h.at[0, pl.ds(R - D, D)], diff_halo.at[0], me_t, me_l + 1, 3, 3)
    prec_back = [
        remote(prec_h.at[0, i], prec_next.at[i], me_t - 1, me_l, 4, next_base + pair_of(i)) for i in range(R)
    ]
    start_back = [
        remote(start_bf.at[i], start_next.at[i], me_t - 1, me_l, 5, next_base + pair_of(i)) for i in range(R)
    ]
    end_on = [remote(end_bf.at[i], end_prev.at[i], me_t + 1, me_l, 6, prev_base + pair_of(i)) for i in range(R)]
    fwd_up, fwd_down, adj_up, adj_down = [], [], [], []
    for k in range(H):
        n, depth = supplied(k)
        first, last = depth - 1, R - depth
        up_src = start_bf.at[first] if n == 0 else fwd_send.at[0, k]
        down_src = start_bf.at[last] if n == 0 else fwd_send.at[1, k]
        fwd_up.append(remote(up_src, fwd_recv.at[1, k], me_t, me_l - 1, 7, fwd_sem[k]))
        fwd_down.append(remote(down_src, fwd_recv.at[0, k], me_t, me_l + 1, 8, fwd_sem[k] + 1))
        adj_up.append(remote(adj_send.at[0, k], adj_recv.at[1, k], me_t, me_l - 1, 9, adj_sem[k]))
        adj_down.append(remote(adj_send.at[1, k], adj_recv.at[0, k], me_t, me_l + 1, 10, adj_sem[k] + 1))

    def go(there, *copies):
        @pl.when(there)
        def _():
            for copy in copies:
                copy.start()

    def sent(there, *waits):
        @pl.when(there)
        def _():
            for out, ref in waits:
                all_sent(out, ref)

    def got(there, *waits):
        @pl.when(there)
        def _():
            for into, ref in waits:
                all_here(into, ref)

    def rows_of(copies, r):
        return [copies[i] for i in pair(r)]

    go(has_up, diff_up)
    go(has_down, diff_down)
    early = [r for r in (1, 0, 2) if r < HALF]
    late = [r for r in range(HALF) if r not in early]
    for r in early:
        go(has_prev, *rows_of(prec_back, r))

    loads["cmap"].wait()
    for r in range(HALF):
        for s, i in enumerate(pair(r)):
            at = (2 * r + s) * LON
            cflat[:, at:at + LON] = cmap[i:i + 1, :]
    high_row = lax.broadcasted_iota(jnp.int32, (C // GL, R * LON), 0)
    in_group[...] = jnp.where(high_row == cflat[...] // GL, 1.0, 0.0).astype(BF16)
    low_lane = lax.rem(lax.broadcasted_iota(jnp.int32, (LON, MEM * GL), 1), GL).astype(F32)
    low_part = jnp.transpose((cmap[...] % GL).astype(F32))
    for r in range(HALF):
        for s, i in enumerate(pair(r)):
            at = (2 * r + s) * LON
            in_lane[at:at + LON] = jnp.where(low_part[:, i:i + 1] == low_lane, 1.0, 0.0).astype(BF16)
    loads["diff"].wait()

    def widen_diff(value, i):
        wide = value.astype(F32)
        d_buf[i] = wide
        e_buf[i] = 1.0 - 4.0 * wide

    for i in range(R):
        widen_diff(diff[i], i + D)
    loads["pert"].wait()
    loads["incr"].wait()
    loads["m_in"].wait()
    loads["m_out"].wait()
    for n in range(H):
        product = jnp.dot(m_in[n], m_out[n], preferred_element_type=F32)
        both[n] = product.astype(BF16)
        both_t[n] = jnp.transpose(product).astype(BF16)
    loads["obs"].wait()
    loads["innov"].wait()
    loads["prec"].wait()
    step_count = steps_ref[0]

    def put(buf, n, i, value):
        buf[n, i, EDGE:EDGE + LON] = value
        buf[n, i, EDGE - 1:EDGE] = value[LON - 1:LON]
        buf[n, i, EDGE + LON:EDGE + LON + 1] = value[0:1]

    def around(buf, n, i):
        north, south = buf[n, i - 1, EDGE:EDGE + LON], buf[n, i + 1, EDGE:EDGE + LON]
        west, east = buf[n, i, EDGE - 1:EDGE - 1 + LON], buf[n, i, EDGE + 1:EDGE + 1 + LON]
        return (north + south) + (west + east)

    def fwd_row(n, r, value, send=True):
        for s, i in enumerate(pair(r)):
            put(s_buf, n, i + DS, value[s])
        for k in range(H):
            if send and supplied(k) == (n, r + 1):
                if n > 0:
                    for s in range(2):
                        fwd_send[s, k] = value[s].astype(BF16)
                go(has_up, fwd_up[k])
                go(has_down, fwd_down[k])

    row = lax.broadcasted_iota(jnp.int32, (GJ, WIDTH), 0)
    lane = lax.broadcasted_iota(jnp.int32, (GJ, WIDTH), 1)
    own_cell = lax.rem(lane, GJ) == row
    groups = LON // GJ

    def places(r):
        found = []
        for at in range(2 * r * LON, 2 * (r + 1) * LON, LANES):
            index = jnp.broadcast_to(cflat[:, at:at + LANES], (MEM, LANES))
            found.append((index // LANES, index % LANES))
        return found

    placed = [places(r) for r in range(HALF)]
    repeat_row = lax.broadcasted_iota(jnp.int32, (MEM, WIDTH), 0)
    repeat_lane = lax.broadcasted_iota(jnp.int32, (MEM, WIDTH), 1) // GJ
    repeat = jnp.where(repeat_row == repeat_lane, 1.0, 0.0).astype(BF16)

    all_here(0, gathered.at[others])
    weights = jnp.concatenate([gathered[p] for p in range(tm_count)], axis=1)
    def pick(r):
        found = []
        for block, inside in placed[r]:
            value = jnp.zeros((MEM, LANES), F32)
            for c in range(C // LANES):
                taken = jnp.take_along_axis(weights[:, c * LANES:(c + 1) * LANES], inside, axis=1)
                value = jnp.where(block == c, taken, value)
            found.append(jnp.transpose(value))
        return jnp.concatenate(found, axis=0).astype(BF16)

    def begin(r):
        cells = pick(r)
        picked = jnp.dot(cells, repeat, preferred_element_type=F32)
        value = []
        for s, i in enumerate(pair(r)):
            pieces = []
            for g in range(groups):
                at = g * GJ
                block = jnp.where(own_cell, picked[s * LON + at:s * LON + at + GJ], 0.0).astype(BF16)
                members = pert[:, i, at:at + GJ, :].reshape(WIDTH, LEV)
                pieces.append(incr[i, at:at + GJ] + jnp.dot(block, members, preferred_element_type=F32))
            state = jnp.concatenate(pieces, axis=0)
            start[i] = state
            start_bf[i] = state.astype(BF16)
            value.append(state)
        fwd_row(0, r, value)
        go(has_prev, *rows_of(start_back, r))

    def modes(value, both):
        flat = jnp.concatenate([v.astype(BF16) for v in value], axis=0)
        moved = jnp.dot(flat, both, preferred_element_type=F32)
        return [value[s] + moved[s * LON:(s + 1) * LON] for s in range(2)]

    def step(n, r):
        here = [s_buf[n, i + DS, EDGE:EDGE + LON] for i in pair(r)]
        smoothed = [e_buf[i + D] * here[s] + d_buf[i + D] * around(s_buf, n, i + DS) for s, i in enumerate(pair(r))]
        result = modes(smoothed, both[n])
        if n > 0:
            result = [jnp.where(n < step_count, a, b) for a, b in zip(result, here)]
        if n + 1 < H:
            fwd_row(n + 1, r, result)
        else:
            for s, i in enumerate(pair(r)):
                end_buf[i] = result[s]
                end_bf[i] = result[s].astype(BF16)
            go(has_next, *rows_of(end_on, r))

    def fold(r):
        return R - 1 - r if r >= HALF else r

    def needs_state(n, r, found):
        if (n, r) in found:
            return
        found.add((n, r))
        if n == 0 or (r < 0 and n <= -r - 1):
            return
        for near in (r - 1, r, r + 1):
            needs_state(n - 1, fold(near), found)

    wanted = set()
    for r in range(HALF):
        needs_state(H, r, wanted)
    known = set()

    def forward():
        while True:
            ready = [
                (n, r) for n, r in sorted(wanted) if (n, r) not in known and n > 0
                and not (r < 0 and n <= -r - 1)
                and all((n - 1, fold(q)) in known for q in (r - 1, r, r + 1))
            ]
            if not ready:
                return
            for n, r in ready:
                step(n - 1, r)
                known.add((n, r))

    for r in range(HALF):
        begin(r)
        known.add((0, r))
        if r == max(early):
            for q in late:
                go(has_prev, *rows_of(prec_back, q))
        forward()

    wanted_u, wanted_w = set(), set()

    def needs_u(m, r):
        if (m, r) in wanted_u:
            return
        wanted_u.add((m, r))
        if m == 0 or (r < 0 and m <= -r - 1):
            return
        needs_u(m - 1, r)
        for near in (r - 1, r, r + 1):
            needs_w(m - 1, fold(near))

    def needs_w(m, r):
        if (m, r) in wanted_w:
            return
        wanted_w.add((m, r))
        if not (r < 0 and m <= -r - 1):
            needs_u(m, r)

    for r in range(HALF):
        needs_u(H, r)
    known_u, known_w, coupled_at = set(), set(), set()

    def adj_send_row(k, value):
        for s in range(2):
            adj_send[s, k] = value[s].astype(BF16)
        go(has_up, adj_up[k])
        go(has_down, adj_down[k])

    def have_u(m, r, value):
        for s, i in enumerate(pair(r)):
            u_buf[i + D] = value[s]
        known_u.add((m, r))
        for k in range(0, H, 2):
            if r >= 0 and supplied(k) == (m, r + 1):
                adj_send_row(k, value)

    def couple(m, r):
        n = H - 1 - m
        here = [u_buf[i + D] for i in pair(r)]
        coupled = modes(here, both_t[n])
        weighted = [d_buf[i + D] * coupled[s] for s, i in enumerate(pair(r))]
        for s, i in enumerate(pair(r)):
            ec_buf[i + D] = e_buf[i + D] * coupled[s]
            put(w_buf, m, i + DS, weighted[s])
        for k in range(1, H, 2):
            if r >= 0 and supplied(k) == (m, r + 1):
                adj_send_row(k, weighted)

    def settle(m, r):
        value = []
        for s, i in enumerate(pair(r)):
            result = ec_buf[i + D] + around(w_buf, m, i + DS)
            if m < H - 1:
                result = jnp.where(H - 1 - m < step_count, result, u_buf[i + D])
            value.append(result)
        if m + 1 < H:
            have_u(m + 1, r, value)
        else:
            known_u.add((H, r))
            final(r, value)

    level_row = lax.broadcasted_iota(jnp.int32, (MEM * LEV, MEM), 0) // LEV
    level_lane = lax.broadcasted_iota(jnp.int32, (MEM * LEV, MEM), 1)
    own = jnp.where(level_row == level_lane, 1.0, 0.0).astype(BF16)
    copy_row = lax.broadcasted_iota(jnp.int32, (MEM, MEM * GL), 0)
    copy_lane = lax.broadcasted_iota(jnp.int32, (MEM, MEM * GL), 1) // GL
    copies = jnp.where(copy_row == copy_lane, 1.0, 0.0).astype(BF16)
    totals = []

    def final(r, value):
        got(has_prev, (prev_base + r, end_prev.at[pl.ds(0, 2)]))
        terms = []
        for s, i in enumerate(pair(r)):
            total = prec[i].astype(F32) * (start[i] - end_prev[i].astype(F32)) + value[s]
            grad_ref[0, i] = total
            rounded = total.astype(BF16)
            terms.append(jnp.concatenate([pert[k, i] * rounded for k in range(MEM)], axis=1))
        summed = jnp.concatenate([jnp.dot(t, own, preferred_element_type=F32) for t in terms], axis=0)
        spread_cells = jnp.dot(summed.astype(BF16), copies, preferred_element_type=F32).astype(BF16)
        at = 2 * r * LON
        placed_terms = spread_cells * in_lane[at:at + 2 * LON]
        share = jnp.dot(in_group[:, at:at + 2 * LON], placed_terms, preferred_element_type=F32)
        sums_buf[...] = share + sums_buf[...] if totals else share
        totals.append(r)

    def leading(goals):
        need_c, need_s, stack = set(), set(), []
        for m, r in goals:
            stack.append(("c" if (m, r + 1) in [supplied(k) for k in range(1, H, 2)] else "u", m, r))
        while stack:
            kind, m, r = stack.pop()
            if kind == "c" and (m, r) not in need_c:
                need_c.add((m, r))
                stack.append(("u", m, r))
            elif kind == "u" and m > 0 and (m - 1, r) not in need_s:
                need_s.add((m - 1, r))
                stack.extend(("c", m - 1, fold(q)) for q in (r - 1, r, r + 1))
        return need_c, need_s

    def adjoint(goals=None):
        only = leading(goals) if goals else None
        while True:
            ready = [("c", m, r) for m, r in sorted(known_u) if m < H and (m, r) not in coupled_at
                     and ((m, r) in wanted_w or (m + 1, r) in wanted_u)]
            ready += [
                ("s", m - 1, r) for m, r in sorted(wanted_u) if m > 0 and (m, r) not in known_u
                and not (r < 0 and m <= -r - 1) and (m - 1, r) in coupled_at
                and all((m - 1, fold(q)) in known_w for q in (r - 1, r, r + 1))
            ]
            if only:
                ready = [t for t in ready if t[1:] in only[0 if t[0] == "c" else 1]]
            if not ready:
                return
            for kind, m, r in ready:
                if kind == "c":
                    couple(m, r)
                    coupled_at.add((m, r))
                    known_w.add((m, r))
                else:
                    settle(m, r)

    def seed(r):
        value = []
        for i in pair(r):
            end = end_buf[i]
            misfit = obs[i].astype(F32) * (end - innov[i].astype(F32))
            value.append(misfit - prec_next[i].astype(F32) * (start_next[i].astype(F32) - end))
        have_u(0, r, value)

    got(has_down, (2, diff_halo.at[1]))
    got(has_up, (3, diff_halo.at[0]))
    for q in range(1, D + 1):
        widen_diff(diff_halo[0, D - q], D - q)
        widen_diff(diff_halo[1, q - 1], R - 1 + D + q)

    urgent = {(supplied(k)[0], supplied(k)[1] - 1) for k in range(H)}

    def seed_and_send(r):
        got(has_next, (next_base + r, prec_next.at[pl.ds(0, 4)]))
        seed(r)
        adjoint(urgent)

    seeded = []
    for some in early_groups:
        got(has_down, (fwd_sem[some[0]], fwd_recv.at[1, pl.ds(0, len(some))]))
        got(has_up, (fwd_sem[some[0]] + 1, fwd_recv.at[0, pl.ds(0, len(some))]))
        for k in some:
            n, depth = supplied(k)
            fwd_row(n, -depth, [fwd_recv[s, k].astype(F32) for s in range(2)], send=False)
            known.add((n, -depth))
        forward()
        if (H, 1) in known and not seeded:
            seed_and_send(1)
            seeded.append(1)
    for r in range(HALF):
        if r not in seeded:
            seed_and_send(r)
    adjoint()

    for some in late_groups:
        got(has_down, (adj_sem[some[0]], adj_recv.at[1, pl.ds(0, len(some))]))
        got(has_up, (adj_sem[some[0]] + 1, adj_recv.at[0, pl.ds(0, len(some))]))
        for k in some:
            m, depth = supplied(k)
            value = [adj_recv[s, k].astype(F32) for s in range(2)]
            if k % 2 == 0:
                have_u(m, -depth, value)
            else:
                for s, i in enumerate(pair(-depth)):
                    put(w_buf, m, i + DS, value[s])
                known_w.add((m, -depth))
        adjoint()

    for p in range(tm_count):
        term_send[p] = sums_buf[p * HB:(p + 1) * HB]
    for d in range(1, tm_count):
        term(d).start()
    result = term_send[me_t]
    all_here(1, term_recv.at[others])
    for d in range(1, tm_count):
        result = result + term_recv[lax.rem(me_t + d, tm_count)]
    out_row = lax.broadcasted_iota(jnp.int32, (MEM, LANES), 0)
    out_lane = lax.broadcasted_iota(jnp.int32, (MEM, LANES), 1)
    owned = jnp.zeros((MEM, LANES), F32)
    for b in range(0, MEM * GL, LANES):
        where_from = out_row * GL + lax.rem(out_lane, GL) - b
        inside = (where_from >= 0) & (where_from < LANES)
        where_from = jnp.clip(where_from, 0, LANES - 1)
        for h in range(HB):
            source = jnp.broadcast_to(result[h:h + 1, b:b + LANES], (MEM, LANES))
            taken = jnp.take_along_axis(source, where_from, axis=1)
            owned = jnp.where(inside & (out_lane // GL == h), taken, owned)
    gw_ref[:, 0, :] = owned[:, 0:CW] + gathered[me_t]

    all_sent(0, gathered.at[others])
    all_sent(1, term_send.at[others])
    sent(has_up, (2, diff_halo.at[0]), (7, fwd_send.at[0]), (9, adj_send.at[0]))
    sent(has_down, (3, diff_halo.at[1]), (8, fwd_send.at[1]), (10, adj_send.at[1]))
    sent(has_prev, (4, prec_next), (5, start_next))
    sent(has_next, (6, end_prev))


def deliver(grad, owned, grad_h, gw_h, sem):
    copies = [
        pltpu.make_async_copy(grad, grad_h, sem.at[0]),
        pltpu.make_async_copy(owned, gw_h, sem.at[1]),
    ]
    for copy in copies:
        copy.start()
    for copy in copies:
        copy.wait()


def solution(mesh):
    tm_count, lat_count = mesh.shape["tm"], mesh.shape["lat"]

    def body(incr, pert, weight, cmap, steps, diffusion, m_in, m_out, prec, obs, innov):
        _, R, LON, LEV = incr.shape
        MEM, _, CW = weight.shape
        H = m_in.shape[0]
        D = max(H // 2, 1)
        DS = max(supplied(k)[1] for k in range(H))
        C = CW * tm_count
        GL = min(WIDTH // MEM, CW)
        field = lambda rows, kind: pltpu.VMEM((rows, LON, LEV), kind)
        padded = pltpu.VMEM((H, R + 2 * DS, LON + 2 * EDGE, LEV), F32)
        halo = pltpu.VMEM((2, H, LON, LEV), BF16)
        scratch = [
            field(R, F32),
            pltpu.VMEM((MEM, R, LON, LEV), BF16),
            pltpu.VMEM((tm_count, MEM, CW), F32),
            pltpu.VMEM((R, LON), jnp.int32),
            field(R, BF16),
            pltpu.VMEM((2, D, LON, LEV), BF16),
            field(R + 2 * D, F32), field(R + 2 * D, F32),
            pltpu.VMEM(m_in.shape, BF16),
            pltpu.VMEM(m_out.shape, BF16),
            field(R, BF16), field(R, BF16), field(R, BF16),
            pltpu.VMEM((H, LEV, LEV), BF16),
            pltpu.VMEM((H, LEV, LEV), BF16),
            pltpu.VMEM((1, R * LON), jnp.int32),
            pltpu.VMEM((C // GL, MEM * GL), F32),
            pltpu.VMEM((C // GL, R * LON), BF16),
            pltpu.VMEM((R * LON, MEM * GL), BF16),
            field(R, F32), field(R, BF16), padded, padded,
            field(R + 2 * D, F32), field(R + 2 * D, F32),
            field(R, F32), field(R, BF16), field(R, BF16), field(R, BF16), field(R, BF16),
            halo, halo, halo, halo,
            pltpu.VMEM((tm_count, CW // GL, MEM * GL), F32),
            pltpu.VMEM((tm_count, CW // GL, MEM * GL), F32),
            pltpu.SemaphoreType.DMA((10,)),
            pltpu.SemaphoreType.DMA((11,)),
            pltpu.SemaphoreType.DMA((4 + 2 * min(H, 3) + 2 * (-(-H // 2)) + R,)),
        ]

        def run(*refs):
            kernel(tm_count, lat_count, (H, R, LON, LEV, MEM, CW), *refs)

        fixed = [
            pltpu.with_memory_space_constraint(x, pltpu.HBM)
            for x in (incr, pert, weight, cmap, diffusion, m_in, m_out, prec, obs, innov)
        ]
        grad, owned = pl.pallas_call(
            run,
            out_shape=(
                pltpu.VMEM(incr.shape, F32),
                pltpu.VMEM((MEM, 1, CW), F32),
            ),
            in_specs=[pl.BlockSpec(memory_space=pltpu.SMEM)] + [pl.BlockSpec(memory_space=pltpu.HBM)] * 10,
            out_specs=(pl.BlockSpec(memory_space=pltpu.VMEM), pl.BlockSpec(memory_space=pltpu.VMEM)),
            scratch_shapes=scratch,
            compiler_params=pltpu.CompilerParams(
                collective_id=0, has_side_effects=True, vmem_limit_bytes=48 * 1024 * 1024
            ),
        )(steps, *fixed)
        grad = pltpu.with_memory_space_constraint(grad, pltpu.VMEM)
        owned = pltpu.with_memory_space_constraint(owned, pltpu.VMEM)
        return pl.pallas_call(
            deliver,
            out_shape=(
                jax.ShapeDtypeStruct(incr.shape, F32),
                jax.ShapeDtypeStruct((MEM, 1, CW), F32),
            ),
            in_specs=[pl.BlockSpec(memory_space=pltpu.VMEM)] * 2,
            out_specs=(pl.BlockSpec(memory_space=pl.ANY), pl.BlockSpec(memory_space=pl.ANY)),
            scratch_shapes=[pltpu.SemaphoreType.DMA((2,))],
        )(grad, owned)

    return jax.shard_map(
        body,
        mesh=mesh,
        in_specs=(
            P("tm", "lat", None, None),
            P(None, "tm", "lat", None, None),
            P(None, "lat", "tm"),
            P("lat", None),
            P("tm"),
            P("tm", "lat", None, None),
            P(),
            P(),
            P("tm", "lat", None, None),
            P("tm", "lat", None, None),
            P("tm", "lat", None, None),
        ),
        out_specs=(P("tm", "lat", None, None), P(None, "lat", "tm")),
        check_vma=False,
    )
```

```python
import jax
import jax.numpy as jnp
from jax import lax
from jax.experimental import pallas as pl
from jax.experimental.pallas import tpu as pltpu
from jax.sharding import PartitionSpec as P

MESH = pl.DeviceIdType.MESH
F32, BF16 = jnp.float32, jnp.bfloat16
EDGE = 8
LANES = 128
WIDTH = 256


def supplied(k):
    return k // 2, k // 2 + k % 2 + 1


def kernel(
    tm_count, lat_count, sizes,
    steps_ref, incr_h, pert_h, weight_h, cmap_h, diff_h, min_h, mout_h, prec_h, obs_h, innov_h,
    grad_ref, gw_ref,
    incr, pert, gathered, cmap, diff, diff_halo, d_buf, e_buf, m_in, m_out, prec, obs, innov,
    both, both_t, cflat, sums_buf, in_group, in_lane, start, start_bf, s_buf, w_buf, u_buf, ec_buf, end_buf, end_bf, end_prev, start_next, prec_next,
    fwd_send, fwd_recv, adj_send, adj_recv,
    term_send, term_recv, local_sem, send_sem, recv_sem,
):
    H, R, LON, LEV, MEM, CW = sizes
    C = CW * tm_count
    D = diff_halo.shape[1]
    DS = (s_buf.shape[1] - R) // 2
    HALF = R // 2
    GJ = WIDTH // MEM
    GL, HB = min(GJ, CW), CW // min(GJ, CW)
    me_t, me_l = lax.axis_index("tm"), lax.axis_index("lat")
    has_up, has_down = me_l > 0, me_l < lat_count - 1
    has_prev, has_next = me_t > 0, me_t < tm_count - 1
    first_core, second_core = lax.rem(me_t, 2) == 0, lax.rem(me_t, 2) == 1

    def pair(r):
        return (r, R - 1 - r)

    def local(i, src, dst):
        return pltpu.make_async_copy(src, dst, local_sem.at[i])

    def remote(src, dst, tm, lat, out, into):
        return pltpu.make_async_remote_copy(
            src_ref=src, dst_ref=dst, send_sem=send_sem.at[out], recv_sem=recv_sem.at[into],
            device_id=(tm, lat), device_id_type=MESH,
        )

    def all_sent(out, ref):
        remote(ref, ref, me_t, me_l, out, 0).wait_send()

    def all_here(into, ref):
        remote(ref, ref, me_t, me_l, 0, into).wait_recv()

    loads = dict(
        weight=local(0, weight_h.at[:, 0], gathered.at[me_t]),
        cmap=local(1, cmap_h, cmap),
        diff=local(2, diff_h.at[0], diff),
        pert=local(3, pert_h.at[:, 0], pert),
        incr=local(4, incr_h.at[0], incr),
        m_in=local(5, min_h, m_in),
        m_out=local(6, mout_h, m_out),
        obs=local(7, obs_h.at[0], obs),
        innov=local(8, innov_h.at[0], innov),
        prec=local(9, prec_h.at[0], prec),
    )
    barrier = pltpu.get_barrier_semaphore()
    for d in range(1, tm_count):
        pl.semaphore_signal(barrier, inc=1, device_id=(lax.rem(me_t + d, tm_count), me_l), device_id_type=MESH)

    @pl.when(has_up)
    def _():
        pl.semaphore_signal(barrier, inc=1, device_id=(me_t, me_l - 1), device_id_type=MESH)

    @pl.when(has_down)
    def _():
        pl.semaphore_signal(barrier, inc=1, device_id=(me_t, me_l + 1), device_id_type=MESH)

    for copy in loads.values():
        copy.start()

    def clear(side):
        diff_halo[side] = jnp.zeros((D, LON, LEV), BF16)
        fwd_recv[side] = jnp.zeros((H, LON, LEV), BF16)
        adj_recv[side] = jnp.zeros((H, LON, LEV), BF16)

    @pl.when(jnp.logical_not(has_up))
    def _():
        clear(0)

    @pl.when(jnp.logical_not(has_down))
    def _():
        clear(1)

    @pl.when(jnp.logical_not(has_prev))
    def _():
        end_prev[...] = jnp.zeros((R, LON, LEV), BF16)

    @pl.when(jnp.logical_not(has_next))
    def _():
        start_next[...] = jnp.zeros((R, LON, LEV), BF16)
        prec_next[...] = jnp.zeros((R, LON, LEV), BF16)

    loads["weight"].wait()
    pl.semaphore_wait(barrier, tm_count - 1 + has_up.astype(jnp.int32) + has_down.astype(jnp.int32))

    others = pl.ds(0, tm_count - 1)

    def spread(d):
        peer = lax.rem(me_t + d, tm_count)
        return remote(gathered.at[me_t], gathered.at[me_t], peer, me_l, 0, 0)

    def term(d):
        peer = lax.rem(me_t + d, tm_count)
        return remote(term_send.at[peer], term_recv.at[me_t], peer, me_l, 1, 1)

    for d in range(1, tm_count):
        spread(d).start()

    early_groups = [list(range(max(H - 2, 0)))] + [[k] for k in range(max(H - 2, 0), H)]
    adj_order = [1, 0] + list(range(2, H)) if H > 1 else [0]
    late_groups = [adj_order[k:k + 2] for k in range(0, H, 2)]
    early_groups = [g for g in early_groups if g]
    fwd_sem = {k: 4 + 2 * g for g, group in enumerate(early_groups) for k in group}
    adj_base = 4 + 2 * len(early_groups)
    adj_sem = {k: adj_base + 2 * g for g, group in enumerate(late_groups) for k in group}
    next_base = adj_base + 2 * len(late_groups)
    prev_base = next_base + HALF

    def pair_of(i):
        return min(i, R - 1 - i)

    diff_up = remote(diff_h.at[0, pl.ds(0, D)], diff_halo.at[1], me_t, me_l - 1, 2, 2)
    diff_down = remote(diff_h.at[0, pl.ds(R - D, D)], diff_halo.at[0], me_t, me_l + 1, 3, 3)
    prec_back = [
        remote(prec_h.at[0, i], prec_next.at[i], me_t - 1, me_l, 4, next_base + pair_of(i)) for i in range(R)
    ]
    start_back = [
        remote(start_bf.at[i], start_next.at[i], me_t - 1, me_l, 5, next_base + pair_of(i)) for i in range(R)
    ]
    end_on = [remote(end_bf.at[i], end_prev.at[i], me_t + 1, me_l, 6, prev_base + pair_of(i)) for i in range(R)]
    fwd_up, fwd_down, adj_up, adj_down = [], [], [], []
    for k in range(H):
        n, depth = supplied(k)
        first, last = depth - 1, R - depth
        up_src = start_bf.at[first] if n == 0 else fwd_send.at[0, k]
        down_src = start_bf.at[last] if n == 0 else fwd_send.at[1, k]
        fwd_up.append(remote(up_src, fwd_recv.at[1, k], me_t, me_l - 1, 7, fwd_sem[k]))
        fwd_down.append(remote(down_src, fwd_recv.at[0, k], me_t, me_l + 1, 8, fwd_sem[k] + 1))
        adj_up.append(remote(adj_send.at[0, k], adj_recv.at[1, k], me_t, me_l - 1, 9, adj_sem[k]))
        adj_down.append(remote(adj_send.at[1, k], adj_recv.at[0, k], me_t, me_l + 1, 10, adj_sem[k] + 1))

    def go(there, *copies):
        @pl.when(there)
        def _():
            for copy in copies:
                copy.start()

    def sent(there, *waits):
        @pl.when(there)
        def _():
            for out, ref in waits:
                all_sent(out, ref)

    def got(there, *waits):
        @pl.when(there)
        def _():
            for into, ref in waits:
                all_here(into, ref)

    def rows_of(copies, r):
        return [copies[i] for i in pair(r)]

    go(has_up, diff_up)
    go(has_down, diff_down)
    early = [r for r in (1, 0, 2) if r < HALF]
    late = [r for r in range(HALF) if r not in early]
    for r in early:
        go(has_prev, *rows_of(prec_back, r))

    loads["cmap"].wait()
    for r in range(HALF):
        for s, i in enumerate(pair(r)):
            at = (2 * r + s) * LON
            cflat[:, at:at + LON] = cmap[i:i + 1, :]
    high_row = lax.broadcasted_iota(jnp.int32, (C // GL, R * LON), 0)
    in_group[...] = jnp.where(high_row == cflat[...] // GL, 1.0, 0.0).astype(BF16)
    low_lane = lax.rem(lax.broadcasted_iota(jnp.int32, (LON, MEM * GL), 1), GL).astype(F32)
    low_part = jnp.transpose((cmap[...] % GL).astype(F32))
    for r in range(HALF):
        for s, i in enumerate(pair(r)):
            at = (2 * r + s) * LON
            in_lane[at:at + LON] = jnp.where(low_part[:, i:i + 1] == low_lane, 1.0, 0.0).astype(BF16)
    loads["diff"].wait()

    def widen_diff(value, i):
        wide = value.astype(F32)
        d_buf[i] = wide
        e_buf[i] = 1.0 - 4.0 * wide

    for i in range(R):
        widen_diff(diff[i], i + D)
    loads["pert"].wait()
    loads["incr"].wait()
    loads["m_in"].wait()
    loads["m_out"].wait()
    for n in range(H):
        product = jnp.dot(m_in[n], m_out[n], preferred_element_type=F32)
        both[n] = product.astype(BF16)
        both_t[n] = jnp.transpose(product).astype(BF16)
    loads["obs"].wait()
    loads["innov"].wait()
    loads["prec"].wait()
    step_count = steps_ref[0]

    def put(buf, n, i, value):
        buf[n, i, EDGE:EDGE + LON] = value
        buf[n, i, EDGE - 1:EDGE] = value[LON - 1:LON]
        buf[n, i, EDGE + LON:EDGE + LON + 1] = value[0:1]

    def around(buf, n, i):
        north, south = buf[n, i - 1, EDGE:EDGE + LON], buf[n, i + 1, EDGE:EDGE + LON]
        west, east = buf[n, i, EDGE - 1:EDGE - 1 + LON], buf[n, i, EDGE + 1:EDGE + 1 + LON]
        return (north + south) + (west + east)

    def fwd_row(n, r, value, send=True):
        for s, i in enumerate(pair(r)):
            put(s_buf, n, i + DS, value[s])
        for k in range(H):
            if send and supplied(k) == (n, r + 1):
                if n > 0:
                    for s in range(2):
                        fwd_send[s, k] = value[s].astype(BF16)
                go(has_up, fwd_up[k])
                go(has_down, fwd_down[k])

    row = lax.broadcasted_iota(jnp.int32, (GJ, WIDTH), 0)
    lane = lax.broadcasted_iota(jnp.int32, (GJ, WIDTH), 1)
    own_cell = lax.rem(lane, GJ) == row
    groups = LON // GJ

    def places(r):
        found = []
        for at in range(2 * r * LON, 2 * (r + 1) * LON, LANES):
            index = jnp.broadcast_to(cflat[:, at:at + LANES], (MEM, LANES))
            found.append((index // LANES, index % LANES))
        return found

    placed = [places(r) for r in range(HALF)]
    all_here(0, gathered.at[others])
    weights = jnp.concatenate([gathered[p] for p in range(tm_count)], axis=1)
    def pick(r):
        found = []
        for block, inside in placed[r]:
            value = jnp.zeros((MEM, LANES), F32)
            for c in range(C // LANES):
                taken = jnp.take_along_axis(weights[:, c * LANES:(c + 1) * LANES], inside, axis=1)
                value = jnp.where(block == c, taken, value)
            wide = jnp.broadcast_to(value[:, None, :], (MEM, GJ, LANES)).reshape(WIDTH, LANES)
            found.append(jnp.transpose(wide))
        return jnp.concatenate(found, axis=0)

    def begin(r):
        picked = pick(r)
        value = []
        for s, i in enumerate(pair(r)):
            pieces = []
            for g in range(groups):
                at = g * GJ
                block = jnp.where(own_cell, picked[s * LON + at:s * LON + at + GJ], 0.0).astype(BF16)
                members = pert[:, i, at:at + GJ, :].reshape(WIDTH, LEV)
                pieces.append(incr[i, at:at + GJ] + jnp.dot(block, members, preferred_element_type=F32))
            state = jnp.concatenate(pieces, axis=0)
            start[i] = state
            start_bf[i] = state.astype(BF16)
            value.append(state)
        fwd_row(0, r, value)
        go(has_prev, *rows_of(start_back, r))

    def modes(value, both):
        flat = jnp.concatenate([v.astype(BF16) for v in value], axis=0)
        moved = jnp.dot(flat, both, preferred_element_type=F32)
        return [value[s] + moved[s * LON:(s + 1) * LON] for s in range(2)]

    def step(n, r):
        here = [s_buf[n, i + DS, EDGE:EDGE + LON] for i in pair(r)]
        smoothed = [e_buf[i + D] * here[s] + d_buf[i + D] * around(s_buf, n, i + DS) for s, i in enumerate(pair(r))]
        result = modes(smoothed, both[n])
        if n > 0:
            result = [jnp.where(n < step_count, a, b) for a, b in zip(result, here)]
        if n + 1 < H:
            fwd_row(n + 1, r, result)
        else:
            for s, i in enumerate(pair(r)):
                end_buf[i] = result[s]
                end_bf[i] = result[s].astype(BF16)

    def fold(r):
        return R - 1 - r if r >= HALF else r

    def needs_state(n, r, found):
        if (n, r) in found:
            return
        found.add((n, r))
        if n == 0 or (r < 0 and n <= -r - 1):
            return
        for near in (r - 1, r, r + 1):
            needs_state(n - 1, fold(near), found)

    wanted = set()
    for r in range(HALF):
        needs_state(H, r, wanted)
    known = set()

    def forward():
        while True:
            ready = [
                (n, r) for n, r in sorted(wanted) if (n, r) not in known and n > 0
                and not (r < 0 and n <= -r - 1)
                and all((n - 1, fold(q)) in known for q in (r - 1, r, r + 1))
            ]
            if not ready:
                return
            for n, r in ready:
                step(n - 1, r)
                known.add((n, r))

    for r in range(HALF):
        begin(r)
        known.add((0, r))
        if r == max(early):
            for q in late:
                go(has_prev, *rows_of(prec_back, q))
        forward()

    wanted_u, wanted_w = set(), set()

    def needs_u(m, r):
        if (m, r) in wanted_u:
            return
        wanted_u.add((m, r))
        if m == 0 or (r < 0 and m <= -r - 1):
            return
        needs_u(m - 1, r)
        for near in (r - 1, r, r + 1):
            needs_w(m - 1, fold(near))

    def needs_w(m, r):
        if (m, r) in wanted_w:
            return
        wanted_w.add((m, r))
        if not (r < 0 and m <= -r - 1):
            needs_u(m, r)

    for r in range(HALF):
        needs_u(H, r)
    known_u, known_w, coupled_at = set(), set(), set()

    def adj_send_row(k, value):
        for s in range(2):
            adj_send[s, k] = value[s].astype(BF16)
        if k in (2, 3):
            go(jnp.logical_and(has_up, first_core), adj_up[k])
            go(jnp.logical_and(has_down, first_core), adj_down[k])
        else:
            go(has_up, adj_up[k])
            go(has_down, adj_down[k])

    def have_u(m, r, value):
        for s, i in enumerate(pair(r)):
            u_buf[i + D] = value[s]
        known_u.add((m, r))
        for k in range(0, H, 2):
            if r >= 0 and supplied(k) == (m, r + 1):
                adj_send_row(k, value)

    def couple(m, r):
        n = H - 1 - m
        here = [u_buf[i + D] for i in pair(r)]
        coupled = modes(here, both_t[n])
        weighted = [d_buf[i + D] * coupled[s] for s, i in enumerate(pair(r))]
        for s, i in enumerate(pair(r)):
            ec_buf[i + D] = e_buf[i + D] * coupled[s]
            put(w_buf, m, i + DS, weighted[s])
        for k in range(1, H, 2):
            if r >= 0 and supplied(k) == (m, r + 1):
                adj_send_row(k, weighted)

    def settle(m, r):
        value = []
        for s, i in enumerate(pair(r)):
            result = ec_buf[i + D] + around(w_buf, m, i + DS)
            if m < H - 1:
                result = jnp.where(H - 1 - m < step_count, result, u_buf[i + D])
            value.append(result)
        if m + 1 < H:
            have_u(m + 1, r, value)
        else:
            known_u.add((H, r))
            final(r, value)

    level_row = lax.broadcasted_iota(jnp.int32, (MEM * LEV, MEM), 0) // LEV
    level_lane = lax.broadcasted_iota(jnp.int32, (MEM * LEV, MEM), 1)
    own = jnp.where(level_row == level_lane, 1.0, 0.0).astype(BF16)
    copy_row = lax.broadcasted_iota(jnp.int32, (MEM, MEM * GL), 0)
    copy_lane = lax.broadcasted_iota(jnp.int32, (MEM, MEM * GL), 1) // GL
    copies = jnp.where(copy_row == copy_lane, 1.0, 0.0).astype(BF16)
    totals = []

    def final(r, value):
        got(has_prev, (prev_base + r, end_prev.at[pl.ds(0, 2)]))
        terms = []
        for s, i in enumerate(pair(r)):
            total = prec[i].astype(F32) * (start[i] - end_prev[i].astype(F32)) + value[s]
            grad_ref[0, i] = total
            rounded = total.astype(BF16)
            terms.append(jnp.concatenate([pert[k, i] * rounded for k in range(MEM)], axis=1))
        summed = jnp.concatenate([jnp.dot(t, own, preferred_element_type=F32) for t in terms], axis=0)
        spread_cells = jnp.dot(summed.astype(BF16), copies, preferred_element_type=F32).astype(BF16)
        at = 2 * r * LON
        placed_terms = spread_cells * in_lane[at:at + 2 * LON]
        share = jnp.dot(in_group[:, at:at + 2 * LON], placed_terms, preferred_element_type=F32)
        sums_buf[...] = share + sums_buf[...] if totals else share
        totals.append(r)

    def leading(goals):
        need_c, need_s, stack = set(), set(), []
        for m, r in goals:
            stack.append(("c" if (m, r + 1) in [supplied(k) for k in range(1, H, 2)] else "u", m, r))
        while stack:
            kind, m, r = stack.pop()
            if kind == "c" and (m, r) not in need_c:
                need_c.add((m, r))
                stack.append(("u", m, r))
            elif kind == "u" and m > 0 and (m - 1, r) not in need_s:
                need_s.add((m - 1, r))
                stack.extend(("c", m - 1, fold(q)) for q in (r - 1, r, r + 1))
        return need_c, need_s

    def adjoint(goals=None):
        only = leading(goals) if goals else None
        while True:
            ready = [("c", m, r) for m, r in sorted(known_u) if m < H and (m, r) not in coupled_at
                     and ((m, r) in wanted_w or (m + 1, r) in wanted_u)]
            ready += [
                ("s", m - 1, r) for m, r in sorted(wanted_u) if m > 0 and (m, r) not in known_u
                and not (r < 0 and m <= -r - 1) and (m - 1, r) in coupled_at
                and all((m - 1, fold(q)) in known_w for q in (r - 1, r, r + 1))
            ]
            if only:
                ready = [t for t in ready if t[1:] in only[0 if t[0] == "c" else 1]]
            if not ready:
                return
            for kind, m, r in ready:
                if kind == "c":
                    couple(m, r)
                    coupled_at.add((m, r))
                    known_w.add((m, r))
                else:
                    settle(m, r)

    def seed(r):
        value = []
        for i in pair(r):
            end = end_buf[i]
            misfit = obs[i].astype(F32) * (end - innov[i].astype(F32))
            value.append(misfit - prec_next[i].astype(F32) * (start_next[i].astype(F32) - end))
        have_u(0, r, value)

    got(has_down, (2, diff_halo.at[1]))
    got(has_up, (3, diff_halo.at[0]))
    for q in range(1, D + 1):
        widen_diff(diff_halo[0, D - q], D - q)
        widen_diff(diff_halo[1, q - 1], R - 1 + D + q)

    urgent = {(supplied(k)[0], supplied(k)[1] - 1) for k in range(H)}

    def seed_and_send(r):
        got(has_next, (next_base + r, prec_next.at[pl.ds(0, 4)]))
        seed(r)
        adjoint(urgent)

    seeded = []
    for some in early_groups:
        got(has_down, (fwd_sem[some[0]], fwd_recv.at[1, pl.ds(0, len(some))]))
        got(has_up, (fwd_sem[some[0]] + 1, fwd_recv.at[0, pl.ds(0, len(some))]))
        for k in some:
            n, depth = supplied(k)
            fwd_row(n, -depth, [fwd_recv[s, k].astype(F32) for s in range(2)], send=False)
            known.add((n, -depth))
        forward()
        if (H, 1) in known and not seeded:
            seed_and_send(1)
            seeded.append(1)
    for r in range(HALF):
        if r == HALF - 1:
            for q in reversed(range(HALF)):
                go(has_next, *rows_of(end_on, q))
        if r not in seeded:
            seed_and_send(r)
    adjoint()
    for k in range(H):
        if k in (2, 3):
            go(jnp.logical_and(has_up, second_core), adj_up[k])
            go(jnp.logical_and(has_down, second_core), adj_down[k])

    for some in late_groups:
        got(has_down, (adj_sem[some[0]], adj_recv.at[1, pl.ds(0, len(some))]))
        got(has_up, (adj_sem[some[0]] + 1, adj_recv.at[0, pl.ds(0, len(some))]))
        for k in some:
            m, depth = supplied(k)
            value = [adj_recv[s, k].astype(F32) for s in range(2)]
            if k % 2 == 0:
                have_u(m, -depth, value)
            else:
                for s, i in enumerate(pair(-depth)):
                    put(w_buf, m, i + DS, value[s])
                known_w.add((m, -depth))
        adjoint()

    for p in range(tm_count):
        term_send[p] = sums_buf[p * HB:(p + 1) * HB]
    for d in range(1, tm_count):
        term(d).start()
    result = term_send[me_t]
    all_here(1, term_recv.at[others])
    for d in range(1, tm_count):
        result = result + term_recv[lax.rem(me_t + d, tm_count)]
    out_row = lax.broadcasted_iota(jnp.int32, (MEM, LANES), 0)
    out_lane = lax.broadcasted_iota(jnp.int32, (MEM, LANES), 1)
    owned = jnp.zeros((MEM, LANES), F32)
    for b in range(0, MEM * GL, LANES):
        where_from = out_row * GL + lax.rem(out_lane, GL) - b
        inside = (where_from >= 0) & (where_from < LANES)
        where_from = jnp.clip(where_from, 0, LANES - 1)
        for h in range(HB):
            source = jnp.broadcast_to(result[h:h + 1, b:b + LANES], (MEM, LANES))
            taken = jnp.take_along_axis(source, where_from, axis=1)
            owned = jnp.where(inside & (out_lane // GL == h), taken, owned)
    gw_ref[:, 0, :] = owned[:, 0:CW] + gathered[me_t]

    all_sent(0, gathered.at[others])
    all_sent(1, term_send.at[others])
    sent(has_up, (2, diff_halo.at[0]), (7, fwd_send.at[0]), (9, adj_send.at[0]))
    sent(has_down, (3, diff_halo.at[1]), (8, fwd_send.at[1]), (10, adj_send.at[1]))
    sent(has_prev, (4, prec_next), (5, start_next))
    sent(has_next, (6, end_prev))


def deliver(grad, owned, grad_h, gw_h, sem):
    copies = [
        pltpu.make_async_copy(grad, grad_h, sem.at[0]),
        pltpu.make_async_copy(owned, gw_h, sem.at[1]),
    ]
    for copy in copies:
        copy.start()
    for copy in copies:
        copy.wait()


def solution(mesh):
    tm_count, lat_count = mesh.shape["tm"], mesh.shape["lat"]

    def body(incr, pert, weight, cmap, steps, diffusion, m_in, m_out, prec, obs, innov):
        _, R, LON, LEV = incr.shape
        MEM, _, CW = weight.shape
        H = m_in.shape[0]
        D = max(H // 2, 1)
        DS = max(supplied(k)[1] for k in range(H))
        C = CW * tm_count
        GL = min(WIDTH // MEM, CW)
        field = lambda rows, kind: pltpu.VMEM((rows, LON, LEV), kind)
        padded = pltpu.VMEM((H, R + 2 * DS, LON + 2 * EDGE, LEV), F32)
        halo = pltpu.VMEM((2, H, LON, LEV), BF16)
        scratch = [
            field(R, F32),
            pltpu.VMEM((MEM, R, LON, LEV), BF16),
            pltpu.VMEM((tm_count, MEM, CW), F32),
            pltpu.VMEM((R, LON), jnp.int32),
            field(R, BF16),
            pltpu.VMEM((2, D, LON, LEV), BF16),
            field(R + 2 * D, F32), field(R + 2 * D, F32),
            pltpu.VMEM(m_in.shape, BF16),
            pltpu.VMEM(m_out.shape, BF16),
            field(R, BF16), field(R, BF16), field(R, BF16),
            pltpu.VMEM((H, LEV, LEV), BF16),
            pltpu.VMEM((H, LEV, LEV), BF16),
            pltpu.VMEM((1, R * LON), jnp.int32),
            pltpu.VMEM((C // GL, MEM * GL), F32),
            pltpu.VMEM((C // GL, R * LON), BF16),
            pltpu.VMEM((R * LON, MEM * GL), BF16),
            field(R, F32), field(R, BF16), padded, padded,
            field(R + 2 * D, F32), field(R + 2 * D, F32),
            field(R, F32), field(R, BF16), field(R, BF16), field(R, BF16), field(R, BF16),
            halo, halo, halo, halo,
            pltpu.VMEM((tm_count, CW // GL, MEM * GL), F32),
            pltpu.VMEM((tm_count, CW // GL, MEM * GL), F32),
            pltpu.SemaphoreType.DMA((10,)),
            pltpu.SemaphoreType.DMA((11,)),
            pltpu.SemaphoreType.DMA((4 + 2 * min(H, 3) + 2 * (-(-H // 2)) + R,)),
        ]

        def run(*refs):
            kernel(tm_count, lat_count, (H, R, LON, LEV, MEM, CW), *refs)

        fixed = [
            pltpu.with_memory_space_constraint(x, pltpu.HBM)
            for x in (incr, pert, weight, cmap, diffusion, m_in, m_out, prec, obs, innov)
        ]
        grad, owned = pl.pallas_call(
            run,
            out_shape=(
                pltpu.VMEM(incr.shape, F32),
                pltpu.VMEM((MEM, 1, CW), F32),
            ),
            in_specs=[pl.BlockSpec(memory_space=pltpu.SMEM)] + [pl.BlockSpec(memory_space=pltpu.HBM)] * 10,
            out_specs=(pl.BlockSpec(memory_space=pltpu.VMEM), pl.BlockSpec(memory_space=pltpu.VMEM)),
            scratch_shapes=scratch,
            compiler_params=pltpu.CompilerParams(
                collective_id=0, has_side_effects=True, vmem_limit_bytes=48 * 1024 * 1024
            ),
        )(steps, *fixed)
        grad = pltpu.with_memory_space_constraint(grad, pltpu.VMEM)
        owned = pltpu.with_memory_space_constraint(owned, pltpu.VMEM)
        return pl.pallas_call(
            deliver,
            out_shape=(
                jax.ShapeDtypeStruct(incr.shape, F32),
                jax.ShapeDtypeStruct((MEM, 1, CW), F32),
            ),
            in_specs=[pl.BlockSpec(memory_space=pltpu.VMEM)] * 2,
            out_specs=(pl.BlockSpec(memory_space=pl.ANY), pl.BlockSpec(memory_space=pl.ANY)),
            scratch_shapes=[pltpu.SemaphoreType.DMA((2,))],
        )(grad, owned)

    return jax.shard_map(
        body,
        mesh=mesh,
        in_specs=(
            P("tm", "lat", None, None),
            P(None, "tm", "lat", None, None),
            P(None, "lat", "tm"),
            P("lat", None),
            P("tm"),
            P("tm", "lat", None, None),
            P(),
            P(),
            P("tm", "lat", None, None),
            P("tm", "lat", None, None),
            P("tm", "lat", None, None),
        ),
        out_specs=(P("tm", "lat", None, None), P(None, "lat", "tm")),
        check_vma=False,
    )
```

```python
import jax
import jax.numpy as jnp
from jax import lax
from jax.experimental import pallas as pl
from jax.experimental.pallas import tpu as pltpu
from jax.sharding import PartitionSpec as P

MESH = pl.DeviceIdType.MESH
F32, BF16 = jnp.float32, jnp.bfloat16
EDGE = 8
LANES = 128
WIDTH = 256


def supplied(k):
    return k // 2, k // 2 + k % 2 + 1


def kernel(
    tm_count, lat_count, sizes,
    steps_ref, incr_h, pert_h, weight_h, cmap_h, diff_h, min_h, mout_h, prec_h, obs_h, innov_h,
    grad_ref, gw_ref,
    incr, pert, gathered, cmap, diff, diff_halo, d_buf, e_buf, m_in, m_out, prec, obs, innov,
    both, both_t, cflat, sums_buf, in_group, in_lane, start, start_bf, s_buf, w_buf, u_buf, ec_buf, end_buf, end_bf, end_prev, start_next, prec_next,
    fwd_send, fwd_recv, adj_send, adj_recv,
    term_send, term_recv, local_sem, send_sem, recv_sem,
):
    H, R, LON, LEV, MEM, CW = sizes
    C = CW * tm_count
    D = diff_halo.shape[1]
    DS = (s_buf.shape[1] - R) // 2
    HALF = R // 2
    GJ = WIDTH // MEM
    GL, HB = min(GJ, CW), CW // min(GJ, CW)
    me_t, me_l = lax.axis_index("tm"), lax.axis_index("lat")
    has_up, has_down = me_l > 0, me_l < lat_count - 1
    has_prev, has_next = me_t > 0, me_t < tm_count - 1
    first_core, second_core = lax.rem(me_t, 2) == 0, lax.rem(me_t, 2) == 1

    def pair(r):
        return (r, R - 1 - r)

    def local(i, src, dst):
        return pltpu.make_async_copy(src, dst, local_sem.at[i])

    def remote(src, dst, tm, lat, out, into):
        return pltpu.make_async_remote_copy(
            src_ref=src, dst_ref=dst, send_sem=send_sem.at[out], recv_sem=recv_sem.at[into],
            device_id=(tm, lat), device_id_type=MESH,
        )

    def all_sent(out, ref):
        remote(ref, ref, me_t, me_l, out, 0).wait_send()

    def all_here(into, ref):
        remote(ref, ref, me_t, me_l, 0, into).wait_recv()

    loads = dict(
        weight=local(0, weight_h.at[:, 0], gathered.at[me_t]),
        cmap=local(1, cmap_h, cmap),
        diff=local(2, diff_h.at[0], diff),
        pert=local(3, pert_h.at[:, 0], pert),
        incr=local(4, incr_h.at[0], incr),
        m_in=local(5, min_h, m_in),
        m_out=local(6, mout_h, m_out),
        obs=local(7, obs_h.at[0], obs),
        innov=local(8, innov_h.at[0], innov),
        prec=local(9, prec_h.at[0], prec),
    )
    barrier = pltpu.get_barrier_semaphore()
    for d in range(1, tm_count):
        pl.semaphore_signal(barrier, inc=1, device_id=(lax.rem(me_t + d, tm_count), me_l), device_id_type=MESH)

    @pl.when(has_up)
    def _():
        pl.semaphore_signal(barrier, inc=1, device_id=(me_t, me_l - 1), device_id_type=MESH)

    @pl.when(has_down)
    def _():
        pl.semaphore_signal(barrier, inc=1, device_id=(me_t, me_l + 1), device_id_type=MESH)

    for copy in loads.values():
        copy.start()

    def clear(side):
        diff_halo[side] = jnp.zeros((D, LON, LEV), BF16)
        fwd_recv[side] = jnp.zeros((H, LON, LEV), BF16)
        adj_recv[side] = jnp.zeros((H, LON, LEV), BF16)

    @pl.when(jnp.logical_not(has_up))
    def _():
        clear(0)

    @pl.when(jnp.logical_not(has_down))
    def _():
        clear(1)

    @pl.when(jnp.logical_not(has_prev))
    def _():
        end_prev[...] = jnp.zeros((R, LON, LEV), BF16)

    @pl.when(jnp.logical_not(has_next))
    def _():
        start_next[...] = jnp.zeros((R, LON, LEV), BF16)
        prec_next[...] = jnp.zeros((R, LON, LEV), BF16)

    loads["weight"].wait()
    pl.semaphore_wait(barrier, tm_count - 1 + has_up.astype(jnp.int32) + has_down.astype(jnp.int32))

    others = pl.ds(0, tm_count - 1)

    def spread(d):
        peer = lax.rem(me_t + d, tm_count)
        return remote(gathered.at[me_t], gathered.at[me_t], peer, me_l, 0, 0)

    def term(d):
        peer = lax.rem(me_t + d, tm_count)
        return remote(term_send.at[peer], term_recv.at[me_t], peer, me_l, 1, 1)

    for d in range(1, tm_count):
        spread(d).start()

    early_groups = [list(range(max(H - 2, 0)))] + [[k] for k in range(max(H - 2, 0), H)]
    adj_order = [1, 0] + list(range(2, H)) if H > 1 else [0]
    late_groups = [adj_order[k:k + 2] for k in range(0, H, 2)]
    early_groups = [g for g in early_groups if g]
    fwd_sem = {k: 4 + 2 * g for g, group in enumerate(early_groups) for k in group}
    adj_base = 4 + 2 * len(early_groups)
    adj_sem = {k: adj_base + 2 * g for g, group in enumerate(late_groups) for k in group}
    next_base = adj_base + 2 * len(late_groups)
    prev_base = next_base + HALF

    def pair_of(i):
        return min(i, R - 1 - i)

    diff_up = remote(diff_h.at[0, pl.ds(0, D)], diff_halo.at[1], me_t, me_l - 1, 2, 2)
    diff_down = remote(diff_h.at[0, pl.ds(R - D, D)], diff_halo.at[0], me_t, me_l + 1, 3, 3)
    prec_back = [
        remote(prec_h.at[0, i], prec_next.at[i], me_t - 1, me_l, 4, next_base + pair_of(i)) for i in range(R)
    ]
    start_back = [
        remote(start_bf.at[i], start_next.at[i], me_t - 1, me_l, 5, next_base + pair_of(i)) for i in range(R)
    ]
    end_on = [remote(end_bf.at[i], end_prev.at[i], me_t + 1, me_l, 6, prev_base + pair_of(i)) for i in range(R)]
    fwd_up, fwd_down, adj_up, adj_down = [], [], [], []
    for k in range(H):
        n, depth = supplied(k)
        first, last = depth - 1, R - depth
        up_src = start_bf.at[first] if n == 0 else fwd_send.at[0, k]
        down_src = start_bf.at[last] if n == 0 else fwd_send.at[1, k]
        fwd_up.append(remote(up_src, fwd_recv.at[1, k], me_t, me_l - 1, 7, fwd_sem[k]))
        fwd_down.append(remote(down_src, fwd_recv.at[0, k], me_t, me_l + 1, 8, fwd_sem[k] + 1))
        adj_up.append(remote(adj_send.at[0, k], adj_recv.at[1, k], me_t, me_l - 1, 9, adj_sem[k]))
        adj_down.append(remote(adj_send.at[1, k], adj_recv.at[0, k], me_t, me_l + 1, 10, adj_sem[k] + 1))

    def go(there, *copies):
        @pl.when(there)
        def _():
            for copy in copies:
                copy.start()

    def sent(there, *waits):
        @pl.when(there)
        def _():
            for out, ref in waits:
                all_sent(out, ref)

    def got(there, *waits):
        @pl.when(there)
        def _():
            for into, ref in waits:
                all_here(into, ref)

    def rows_of(copies, r):
        return [copies[i] for i in pair(r)]

    go(has_up, diff_up)
    go(has_down, diff_down)
    early = [r for r in (1, 0, 2) if r < HALF]
    late = [r for r in range(HALF) if r not in early]
    for r in early:
        go(has_prev, *rows_of(prec_back, r))

    loads["cmap"].wait()
    for r in range(HALF):
        for s, i in enumerate(pair(r)):
            at = (2 * r + s) * LON
            cflat[:, at:at + LON] = cmap[i:i + 1, :]
    high_row = lax.broadcasted_iota(jnp.int32, (C // GL, R * LON), 0)
    in_group[...] = jnp.where(high_row == cflat[...] // GL, 1.0, 0.0).astype(BF16)
    low_lane = lax.rem(lax.broadcasted_iota(jnp.int32, (LON, MEM * GL), 1), GL).astype(F32)
    low_part = jnp.transpose((cmap[...] % GL).astype(F32))
    for r in range(HALF):
        for s, i in enumerate(pair(r)):
            at = (2 * r + s) * LON
            in_lane[at:at + LON] = jnp.where(low_part[:, i:i + 1] == low_lane, 1.0, 0.0).astype(BF16)
    loads["diff"].wait()

    def widen_diff(value, i):
        wide = value.astype(F32)
        d_buf[i] = wide
        e_buf[i] = 1.0 - 4.0 * wide

    for i in range(R):
        widen_diff(diff[i], i + D)
    loads["pert"].wait()
    loads["incr"].wait()
    loads["m_in"].wait()
    loads["m_out"].wait()
    for n in range(H):
        product = jnp.dot(m_in[n], m_out[n], preferred_element_type=F32)
        both[n] = product.astype(BF16)
        both_t[n] = jnp.transpose(product).astype(BF16)
    loads["obs"].wait()
    loads["innov"].wait()
    loads["prec"].wait()
    step_count = steps_ref[0]

    def put(buf, n, i, value):
        buf[n, i, EDGE:EDGE + LON] = value
        buf[n, i, EDGE - 1:EDGE] = value[LON - 1:LON]
        buf[n, i, EDGE + LON:EDGE + LON + 1] = value[0:1]

    def around(buf, n, i):
        north, south = buf[n, i - 1, EDGE:EDGE + LON], buf[n, i + 1, EDGE:EDGE + LON]
        west, east = buf[n, i, EDGE - 1:EDGE - 1 + LON], buf[n, i, EDGE + 1:EDGE + 1 + LON]
        return (north + south) + (west + east)

    def fwd_row(n, r, value, send=True):
        for s, i in enumerate(pair(r)):
            put(s_buf, n, i + DS, value[s])
        for k in range(H):
            if send and supplied(k) == (n, r + 1):
                if n > 0:
                    for s in range(2):
                        fwd_send[s, k] = value[s].astype(BF16)
                if k in (1, 2, 3):
                    go(jnp.logical_and(has_up, first_core), fwd_up[k])
                    go(jnp.logical_and(has_down, first_core), fwd_down[k])
                else:
                    go(has_up, fwd_up[k])
                    go(has_down, fwd_down[k])

    row = lax.broadcasted_iota(jnp.int32, (GJ, WIDTH), 0)
    lane = lax.broadcasted_iota(jnp.int32, (GJ, WIDTH), 1)
    own_cell = lax.rem(lane, GJ) == row
    groups = LON // GJ

    def places(r):
        found = []
        for at in range(2 * r * LON, 2 * (r + 1) * LON, LANES):
            index = jnp.broadcast_to(cflat[:, at:at + LANES], (MEM, LANES))
            found.append((index // LANES, index % LANES))
        return found

    placed = [places(r) for r in range(HALF)]
    all_here(0, gathered.at[others])
    weights = jnp.concatenate([gathered[p] for p in range(tm_count)], axis=1)
    def pick(r):
        found = []
        for block, inside in placed[r]:
            value = jnp.zeros((MEM, LANES), F32)
            for c in range(C // LANES):
                taken = jnp.take_along_axis(weights[:, c * LANES:(c + 1) * LANES], inside, axis=1)
                value = jnp.where(block == c, taken, value)
            wide = jnp.broadcast_to(value[:, None, :], (MEM, GJ, LANES)).reshape(WIDTH, LANES)
            found.append(jnp.transpose(wide))
        return jnp.concatenate(found, axis=0)

    def begin(r):
        picked = pick(r)
        value = []
        for s, i in enumerate(pair(r)):
            pieces = []
            for g in range(groups):
                at = g * GJ
                block = jnp.where(own_cell, picked[s * LON + at:s * LON + at + GJ], 0.0).astype(BF16)
                members = pert[:, i, at:at + GJ, :].reshape(WIDTH, LEV)
                pieces.append(incr[i, at:at + GJ] + jnp.dot(block, members, preferred_element_type=F32))
            state = jnp.concatenate(pieces, axis=0)
            start[i] = state
            start_bf[i] = state.astype(BF16)
            value.append(state)
        fwd_row(0, r, value)
        go(has_prev, *rows_of(start_back, r))

    def modes(value, both):
        flat = jnp.concatenate([v.astype(BF16) for v in value], axis=0)
        moved = jnp.dot(flat, both, preferred_element_type=F32)
        return [value[s] + moved[s * LON:(s + 1) * LON] for s in range(2)]

    def step(n, r):
        here = [s_buf[n, i + DS, EDGE:EDGE + LON] for i in pair(r)]
        smoothed = [e_buf[i + D] * here[s] + d_buf[i + D] * around(s_buf, n, i + DS) for s, i in enumerate(pair(r))]
        result = modes(smoothed, both[n])
        if n > 0:
            result = [jnp.where(n < step_count, a, b) for a, b in zip(result, here)]
        if n + 1 < H:
            fwd_row(n + 1, r, result)
        else:
            for s, i in enumerate(pair(r)):
                end_buf[i] = result[s]
                end_bf[i] = result[s].astype(BF16)

    def fold(r):
        return R - 1 - r if r >= HALF else r

    def needs_state(n, r, found):
        if (n, r) in found:
            return
        found.add((n, r))
        if n == 0 or (r < 0 and n <= -r - 1):
            return
        for near in (r - 1, r, r + 1):
            needs_state(n - 1, fold(near), found)

    wanted = set()
    for r in range(HALF):
        needs_state(H, r, wanted)
    known = set()

    def forward():
        while True:
            ready = [
                (n, r) for n, r in sorted(wanted) if (n, r) not in known and n > 0
                and not (r < 0 and n <= -r - 1)
                and all((n - 1, fold(q)) in known for q in (r - 1, r, r + 1))
            ]
            if not ready:
                return
            for n, r in ready:
                step(n - 1, r)
                known.add((n, r))

    for r in range(HALF):
        begin(r)
        known.add((0, r))
        if r == max(early):
            for q in late:
                go(has_prev, *rows_of(prec_back, q))
        forward()

    for k in range(H):
        if k in (1, 2, 3):
            go(jnp.logical_and(has_up, second_core), fwd_up[k])
            go(jnp.logical_and(has_down, second_core), fwd_down[k])

    wanted_u, wanted_w = set(), set()

    def needs_u(m, r):
        if (m, r) in wanted_u:
            return
        wanted_u.add((m, r))
        if m == 0 or (r < 0 and m <= -r - 1):
            return
        needs_u(m - 1, r)
        for near in (r - 1, r, r + 1):
            needs_w(m - 1, fold(near))

    def needs_w(m, r):
        if (m, r) in wanted_w:
            return
        wanted_w.add((m, r))
        if not (r < 0 and m <= -r - 1):
            needs_u(m, r)

    for r in range(HALF):
        needs_u(H, r)
    known_u, known_w, coupled_at = set(), set(), set()

    def adj_send_row(k, value):
        for s in range(2):
            adj_send[s, k] = value[s].astype(BF16)
        if k in (2, 3):
            go(jnp.logical_and(has_up, first_core), adj_up[k])
            go(jnp.logical_and(has_down, first_core), adj_down[k])
        else:
            go(has_up, adj_up[k])
            go(has_down, adj_down[k])

    def have_u(m, r, value):
        for s, i in enumerate(pair(r)):
            u_buf[i + D] = value[s]
        known_u.add((m, r))
        for k in range(0, H, 2):
            if r >= 0 and supplied(k) == (m, r + 1):
                adj_send_row(k, value)

    def couple(m, r):
        n = H - 1 - m
        here = [u_buf[i + D] for i in pair(r)]
        coupled = modes(here, both_t[n])
        weighted = [d_buf[i + D] * coupled[s] for s, i in enumerate(pair(r))]
        for s, i in enumerate(pair(r)):
            ec_buf[i + D] = e_buf[i + D] * coupled[s]
            put(w_buf, m, i + DS, weighted[s])
        for k in range(1, H, 2):
            if r >= 0 and supplied(k) == (m, r + 1):
                adj_send_row(k, weighted)

    def settle(m, r):
        value = []
        for s, i in enumerate(pair(r)):
            result = ec_buf[i + D] + around(w_buf, m, i + DS)
            if m < H - 1:
                result = jnp.where(H - 1 - m < step_count, result, u_buf[i + D])
            value.append(result)
        if m + 1 < H:
            have_u(m + 1, r, value)
        else:
            known_u.add((H, r))
            final(r, value)

    level_row = lax.broadcasted_iota(jnp.int32, (MEM * LEV, MEM), 0) // LEV
    level_lane = lax.broadcasted_iota(jnp.int32, (MEM * LEV, MEM), 1)
    own = jnp.where(level_row == level_lane, 1.0, 0.0).astype(BF16)
    copy_row = lax.broadcasted_iota(jnp.int32, (MEM, MEM * GL), 0)
    copy_lane = lax.broadcasted_iota(jnp.int32, (MEM, MEM * GL), 1) // GL
    copies = jnp.where(copy_row == copy_lane, 1.0, 0.0).astype(BF16)
    totals = []

    def final(r, value):
        got(has_prev, (prev_base + r, end_prev.at[pl.ds(0, 2)]))
        terms = []
        for s, i in enumerate(pair(r)):
            total = prec[i].astype(F32) * (start[i] - end_prev[i].astype(F32)) + value[s]
            grad_ref[0, i] = total
            rounded = total.astype(BF16)
            terms.append(jnp.concatenate([pert[k, i] * rounded for k in range(MEM)], axis=1))
        summed = jnp.concatenate([jnp.dot(t, own, preferred_element_type=F32) for t in terms], axis=0)
        spread_cells = jnp.dot(summed.astype(BF16), copies, preferred_element_type=F32).astype(BF16)
        at = 2 * r * LON
        placed_terms = spread_cells * in_lane[at:at + 2 * LON]
        share = jnp.dot(in_group[:, at:at + 2 * LON], placed_terms, preferred_element_type=F32)
        sums_buf[...] = share + sums_buf[...] if totals else share
        totals.append(r)

    def leading(goals):
        need_c, need_s, stack = set(), set(), []
        for m, r in goals:
            stack.append(("c" if (m, r + 1) in [supplied(k) for k in range(1, H, 2)] else "u", m, r))
        while stack:
            kind, m, r = stack.pop()
            if kind == "c" and (m, r) not in need_c:
                need_c.add((m, r))
                stack.append(("u", m, r))
            elif kind == "u" and m > 0 and (m - 1, r) not in need_s:
                need_s.add((m - 1, r))
                stack.extend(("c", m - 1, fold(q)) for q in (r - 1, r, r + 1))
        return need_c, need_s

    def adjoint(goals=None):
        only = leading(goals) if goals else None
        while True:
            ready = [("c", m, r) for m, r in sorted(known_u) if m < H and (m, r) not in coupled_at
                     and ((m, r) in wanted_w or (m + 1, r) in wanted_u)]
            ready += [
                ("s", m - 1, r) for m, r in sorted(wanted_u) if m > 0 and (m, r) not in known_u
                and not (r < 0 and m <= -r - 1) and (m - 1, r) in coupled_at
                and all((m - 1, fold(q)) in known_w for q in (r - 1, r, r + 1))
            ]
            if only:
                ready = [t for t in ready if t[1:] in only[0 if t[0] == "c" else 1]]
            if not ready:
                return
            for kind, m, r in ready:
                if kind == "c":
                    couple(m, r)
                    coupled_at.add((m, r))
                    known_w.add((m, r))
                else:
                    settle(m, r)

    def seed(r):
        value = []
        for i in pair(r):
            end = end_buf[i]
            misfit = obs[i].astype(F32) * (end - innov[i].astype(F32))
            value.append(misfit - prec_next[i].astype(F32) * (start_next[i].astype(F32) - end))
        have_u(0, r, value)

    got(has_down, (2, diff_halo.at[1]))
    got(has_up, (3, diff_halo.at[0]))
    for q in range(1, D + 1):
        widen_diff(diff_halo[0, D - q], D - q)
        widen_diff(diff_halo[1, q - 1], R - 1 + D + q)

    urgent = {(supplied(k)[0], supplied(k)[1] - 1) for k in range(H)}

    def seed_and_send(r):
        got(has_next, (next_base + r, prec_next.at[pl.ds(0, 4)]))
        seed(r)
        adjoint(urgent)

    seeded = []
    for some in early_groups:
        got(has_down, (fwd_sem[some[0]], fwd_recv.at[1, pl.ds(0, len(some))]))
        got(has_up, (fwd_sem[some[0]] + 1, fwd_recv.at[0, pl.ds(0, len(some))]))
        for k in some:
            n, depth = supplied(k)
            fwd_row(n, -depth, [fwd_recv[s, k].astype(F32) for s in range(2)], send=False)
            known.add((n, -depth))
        forward()
        if (H, 1) in known and not seeded:
            seed_and_send(1)
            seeded.append(1)
    for r in range(HALF):
        if r == HALF - 1:
            for q in reversed(range(HALF)):
                go(has_next, *rows_of(end_on, q))
        if r not in seeded:
            seed_and_send(r)
    adjoint()
    for k in range(H):
        if k in (2, 3):
            go(jnp.logical_and(has_up, second_core), adj_up[k])
            go(jnp.logical_and(has_down, second_core), adj_down[k])

    for some in late_groups:
        got(has_down, (adj_sem[some[0]], adj_recv.at[1, pl.ds(0, len(some))]))
        got(has_up, (adj_sem[some[0]] + 1, adj_recv.at[0, pl.ds(0, len(some))]))
        for k in some:
            m, depth = supplied(k)
            value = [adj_recv[s, k].astype(F32) for s in range(2)]
            if k % 2 == 0:
                have_u(m, -depth, value)
            else:
                for s, i in enumerate(pair(-depth)):
                    put(w_buf, m, i + DS, value[s])
                known_w.add((m, -depth))
        adjoint()

    for p in range(tm_count):
        term_send[p] = sums_buf[p * HB:(p + 1) * HB]
    for d in range(1, tm_count):
        term(d).start()
    result = term_send[me_t]
    all_here(1, term_recv.at[others])
    for d in range(1, tm_count):
        result = result + term_recv[lax.rem(me_t + d, tm_count)]
    out_row = lax.broadcasted_iota(jnp.int32, (MEM, LANES), 0)
    out_lane = lax.broadcasted_iota(jnp.int32, (MEM, LANES), 1)
    owned = jnp.zeros((MEM, LANES), F32)
    for b in range(0, MEM * GL, LANES):
        where_from = out_row * GL + lax.rem(out_lane, GL) - b
        inside = (where_from >= 0) & (where_from < LANES)
        where_from = jnp.clip(where_from, 0, LANES - 1)
        for h in range(HB):
            source = jnp.broadcast_to(result[h:h + 1, b:b + LANES], (MEM, LANES))
            taken = jnp.take_along_axis(source, where_from, axis=1)
            owned = jnp.where(inside & (out_lane // GL == h), taken, owned)
    gw_ref[:, 0, :] = owned[:, 0:CW] + gathered[me_t]

    all_sent(0, gathered.at[others])
    all_sent(1, term_send.at[others])
    sent(has_up, (2, diff_halo.at[0]), (7, fwd_send.at[0]), (9, adj_send.at[0]))
    sent(has_down, (3, diff_halo.at[1]), (8, fwd_send.at[1]), (10, adj_send.at[1]))
    sent(has_prev, (4, prec_next), (5, start_next))
    sent(has_next, (6, end_prev))


def deliver(grad, owned, grad_h, gw_h, sem):
    copies = [
        pltpu.make_async_copy(grad, grad_h, sem.at[0]),
        pltpu.make_async_copy(owned, gw_h, sem.at[1]),
    ]
    for copy in copies:
        copy.start()
    for copy in copies:
        copy.wait()


def solution(mesh):
    tm_count, lat_count = mesh.shape["tm"], mesh.shape["lat"]

    def body(incr, pert, weight, cmap, steps, diffusion, m_in, m_out, prec, obs, innov):
        _, R, LON, LEV = incr.shape
        MEM, _, CW = weight.shape
        H = m_in.shape[0]
        D = max(H // 2, 1)
        DS = max(supplied(k)[1] for k in range(H))
        C = CW * tm_count
        GL = min(WIDTH // MEM, CW)
        field = lambda rows, kind: pltpu.VMEM((rows, LON, LEV), kind)
        padded = pltpu.VMEM((H, R + 2 * DS, LON + 2 * EDGE, LEV), F32)
        halo = pltpu.VMEM((2, H, LON, LEV), BF16)
        scratch = [
            field(R, F32),
            pltpu.VMEM((MEM, R, LON, LEV), BF16),
            pltpu.VMEM((tm_count, MEM, CW), F32),
            pltpu.VMEM((R, LON), jnp.int32),
            field(R, BF16),
            pltpu.VMEM((2, D, LON, LEV), BF16),
            field(R + 2 * D, F32), field(R + 2 * D, F32),
            pltpu.VMEM(m_in.shape, BF16),
            pltpu.VMEM(m_out.shape, BF16),
            field(R, BF16), field(R, BF16), field(R, BF16),
            pltpu.VMEM((H, LEV, LEV), BF16),
            pltpu.VMEM((H, LEV, LEV), BF16),
            pltpu.VMEM((1, R * LON), jnp.int32),
            pltpu.VMEM((C // GL, MEM * GL), F32),
            pltpu.VMEM((C // GL, R * LON), BF16),
            pltpu.VMEM((R * LON, MEM * GL), BF16),
            field(R, F32), field(R, BF16), padded, padded,
            field(R + 2 * D, F32), field(R + 2 * D, F32),
            field(R, F32), field(R, BF16), field(R, BF16), field(R, BF16), field(R, BF16),
            halo, halo, halo, halo,
            pltpu.VMEM((tm_count, CW // GL, MEM * GL), F32),
            pltpu.VMEM((tm_count, CW // GL, MEM * GL), F32),
            pltpu.SemaphoreType.DMA((10,)),
            pltpu.SemaphoreType.DMA((11,)),
            pltpu.SemaphoreType.DMA((4 + 2 * min(H, 3) + 2 * (-(-H // 2)) + R,)),
        ]

        def run(*refs):
            kernel(tm_count, lat_count, (H, R, LON, LEV, MEM, CW), *refs)

        fixed = [
            pltpu.with_memory_space_constraint(x, pltpu.HBM)
            for x in (incr, pert, weight, cmap, diffusion, m_in, m_out, prec, obs, innov)
        ]
        grad, owned = pl.pallas_call(
            run,
            out_shape=(
                pltpu.VMEM(incr.shape, F32),
                pltpu.VMEM((MEM, 1, CW), F32),
            ),
            in_specs=[pl.BlockSpec(memory_space=pltpu.SMEM)] + [pl.BlockSpec(memory_space=pltpu.HBM)] * 10,
            out_specs=(pl.BlockSpec(memory_space=pltpu.VMEM), pl.BlockSpec(memory_space=pltpu.VMEM)),
            scratch_shapes=scratch,
            compiler_params=pltpu.CompilerParams(
                collective_id=0, has_side_effects=True, vmem_limit_bytes=48 * 1024 * 1024
            ),
        )(steps, *fixed)
        grad = pltpu.with_memory_space_constraint(grad, pltpu.VMEM)
        owned = pltpu.with_memory_space_constraint(owned, pltpu.VMEM)
        return pl.pallas_call(
            deliver,
            out_shape=(
                jax.ShapeDtypeStruct(incr.shape, F32),
                jax.ShapeDtypeStruct((MEM, 1, CW), F32),
            ),
            in_specs=[pl.BlockSpec(memory_space=pltpu.VMEM)] * 2,
            out_specs=(pl.BlockSpec(memory_space=pl.ANY), pl.BlockSpec(memory_space=pl.ANY)),
            scratch_shapes=[pltpu.SemaphoreType.DMA((2,))],
        )(grad, owned)

    return jax.shard_map(
        body,
        mesh=mesh,
        in_specs=(
            P("tm", "lat", None, None),
            P(None, "tm", "lat", None, None),
            P(None, "lat", "tm"),
            P("lat", None),
            P("tm"),
            P("tm", "lat", None, None),
            P(),
            P(),
            P("tm", "lat", None, None),
            P("tm", "lat", None, None),
            P("tm", "lat", None, None),
        ),
        out_specs=(P("tm", "lat", None, None), P(None, "lat", "tm")),
        check_vma=False,
    )
```

```python
import jax
import jax.numpy as jnp
from jax import lax
from jax.experimental import pallas as pl
from jax.experimental.pallas import tpu as pltpu
from jax.sharding import PartitionSpec as P

MESH = pl.DeviceIdType.MESH
F32, BF16 = jnp.float32, jnp.bfloat16
EDGE = 8
LANES = 128
WIDTH = 256


def supplied(k):
    return k // 2, k // 2 + k % 2 + 1


def kernel(
    tm_count, lat_count, sizes,
    steps_ref, incr_h, pert_h, weight_h, cmap_h, diff_h, min_h, mout_h, prec_h, obs_h, innov_h,
    grad_ref, gw_ref,
    incr, pert, gathered, cmap, diff, diff_halo, d_buf, e_buf, m_in, m_out, prec, obs, innov,
    both, both_t, cflat, sums_buf, in_group, in_lane, start, start_bf, s_buf, w_buf, u_buf, ec_buf, end_buf, end_bf, end_prev, start_next, prec_next,
    fwd_send, fwd_recv, adj_send, adj_recv,
    term_send, term_recv, local_sem, send_sem, recv_sem,
):
    H, R, LON, LEV, MEM, CW = sizes
    C = CW * tm_count
    D = diff_halo.shape[1]
    DS = (s_buf.shape[1] - R) // 2
    HALF = R // 2
    GJ = WIDTH // MEM
    GL, HB = min(GJ, CW), CW // min(GJ, CW)
    me_t, me_l = lax.axis_index("tm"), lax.axis_index("lat")
    has_up, has_down = me_l > 0, me_l < lat_count - 1
    has_prev, has_next = me_t > 0, me_t < tm_count - 1
    first_core, second_core = lax.rem(me_t, 2) == 0, lax.rem(me_t, 2) == 1

    def pair(r):
        return (r, R - 1 - r)

    def local(i, src, dst):
        return pltpu.make_async_copy(src, dst, local_sem.at[i])

    def remote(src, dst, tm, lat, out, into):
        return pltpu.make_async_remote_copy(
            src_ref=src, dst_ref=dst, send_sem=send_sem.at[out], recv_sem=recv_sem.at[into],
            device_id=(tm, lat), device_id_type=MESH,
        )

    def all_sent(out, ref):
        remote(ref, ref, me_t, me_l, out, 0).wait_send()

    def all_here(into, ref):
        remote(ref, ref, me_t, me_l, 0, into).wait_recv()

    loads = dict(
        weight=local(0, weight_h.at[:, 0], gathered.at[me_t]),
        cmap=local(1, cmap_h, cmap),
        diff=local(2, diff_h.at[0], diff),
        pert=local(3, pert_h.at[:, 0], pert),
        incr=local(4, incr_h.at[0], incr),
        m_in=local(5, min_h, m_in),
        m_out=local(6, mout_h, m_out),
        obs=local(7, obs_h.at[0], obs),
        innov=local(8, innov_h.at[0], innov),
        prec=local(9, prec_h.at[0], prec),
    )
    barrier = pltpu.get_barrier_semaphore()
    for d in range(1, tm_count):
        pl.semaphore_signal(barrier, inc=1, device_id=(lax.rem(me_t + d, tm_count), me_l), device_id_type=MESH)

    @pl.when(has_up)
    def _():
        pl.semaphore_signal(barrier, inc=1, device_id=(me_t, me_l - 1), device_id_type=MESH)

    @pl.when(has_down)
    def _():
        pl.semaphore_signal(barrier, inc=1, device_id=(me_t, me_l + 1), device_id_type=MESH)

    for copy in loads.values():
        copy.start()

    def clear(side):
        diff_halo[side] = jnp.zeros((D, LON, LEV), BF16)
        fwd_recv[side] = jnp.zeros((H, LON, LEV), BF16)
        adj_recv[side] = jnp.zeros((H, LON, LEV), BF16)

    @pl.when(jnp.logical_not(has_up))
    def _():
        clear(0)

    @pl.when(jnp.logical_not(has_down))
    def _():
        clear(1)

    @pl.when(jnp.logical_not(has_prev))
    def _():
        end_prev[...] = jnp.zeros((R, LON, LEV), BF16)

    @pl.when(jnp.logical_not(has_next))
    def _():
        start_next[...] = jnp.zeros((R, LON, LEV), BF16)
        prec_next[...] = jnp.zeros((R, LON, LEV), BF16)

    loads["weight"].wait()
    pl.semaphore_wait(barrier, tm_count - 1 + has_up.astype(jnp.int32) + has_down.astype(jnp.int32))

    others = pl.ds(0, tm_count - 1)

    def spread(d):
        peer = lax.rem(me_t + d, tm_count)
        return remote(gathered.at[me_t], gathered.at[me_t], peer, me_l, 0, 0)

    def term(d):
        peer = lax.rem(me_t + d, tm_count)
        return remote(term_send.at[peer], term_recv.at[me_t], peer, me_l, 1, 1)

    for d in range(1, tm_count):
        spread(d).start()

    early_groups = [list(range(max(H - 2, 0)))] + [[k] for k in range(max(H - 2, 0), H)]
    adj_order = [1, 0] + list(range(2, H)) if H > 1 else [0]
    late_groups = [adj_order[k:k + 2] for k in range(0, H, 2)]
    early_groups = [g for g in early_groups if g]
    fwd_sem = {k: 4 + 2 * g for g, group in enumerate(early_groups) for k in group}
    adj_base = 4 + 2 * len(early_groups)
    adj_sem = {k: adj_base + 2 * g for g, group in enumerate(late_groups) for k in group}
    next_base = adj_base + 2 * len(late_groups)
    prev_base = next_base + HALF

    def pair_of(i):
        return min(i, R - 1 - i)

    diff_up = remote(diff_h.at[0, pl.ds(0, D)], diff_halo.at[1], me_t, me_l - 1, 2, 2)
    diff_down = remote(diff_h.at[0, pl.ds(R - D, D)], diff_halo.at[0], me_t, me_l + 1, 3, 3)
    prec_back = [
        remote(prec_h.at[0, i], prec_next.at[i], me_t - 1, me_l, 4, next_base + pair_of(i)) for i in range(R)
    ]
    start_back = [
        remote(start_bf.at[i], start_next.at[i], me_t - 1, me_l, 5, next_base + pair_of(i)) for i in range(R)
    ]
    end_on = [remote(end_bf.at[i], end_prev.at[i], me_t + 1, me_l, 6, prev_base + pair_of(i)) for i in range(R)]
    fwd_up, fwd_down, adj_up, adj_down = [], [], [], []
    for k in range(H):
        n, depth = supplied(k)
        first, last = depth - 1, R - depth
        up_src = start_bf.at[first] if n == 0 else fwd_send.at[0, k]
        down_src = start_bf.at[last] if n == 0 else fwd_send.at[1, k]
        fwd_up.append(remote(up_src, fwd_recv.at[1, k], me_t, me_l - 1, 7, fwd_sem[k]))
        fwd_down.append(remote(down_src, fwd_recv.at[0, k], me_t, me_l + 1, 8, fwd_sem[k] + 1))
        adj_up.append(remote(adj_send.at[0, k], adj_recv.at[1, k], me_t, me_l - 1, 9, adj_sem[k]))
        adj_down.append(remote(adj_send.at[1, k], adj_recv.at[0, k], me_t, me_l + 1, 10, adj_sem[k] + 1))

    def go(there, *copies):
        @pl.when(there)
        def _():
            for copy in copies:
                copy.start()

    def sent(there, *waits):
        @pl.when(there)
        def _():
            for out, ref in waits:
                all_sent(out, ref)

    def got(there, *waits):
        @pl.when(there)
        def _():
            for into, ref in waits:
                all_here(into, ref)

    def rows_of(copies, r):
        return [copies[i] for i in pair(r)]

    go(has_up, diff_up)
    go(has_down, diff_down)
    early = [r for r in (1, 0, 2) if r < HALF]
    late = [r for r in range(HALF) if r not in early]
    for r in early:
        go(has_prev, *rows_of(prec_back, r))

    loads["cmap"].wait()
    for r in range(HALF):
        for s, i in enumerate(pair(r)):
            at = (2 * r + s) * LON
            cflat[:, at:at + LON] = cmap[i:i + 1, :]
    high_row = lax.broadcasted_iota(jnp.int32, (C // GL, R * LON), 0)
    in_group[...] = jnp.where(high_row == cflat[...] // GL, 1.0, 0.0).astype(BF16)
    low_lane = lax.rem(lax.broadcasted_iota(jnp.int32, (LON, MEM * GL), 1), GL).astype(F32)
    low_part = jnp.transpose((cmap[...] % GL).astype(F32))
    for r in range(HALF):
        for s, i in enumerate(pair(r)):
            at = (2 * r + s) * LON
            in_lane[at:at + LON] = jnp.where(low_part[:, i:i + 1] == low_lane, 1.0, 0.0).astype(BF16)
    loads["diff"].wait()

    def widen_diff(value, i):
        wide = value.astype(F32)
        d_buf[i] = wide
        e_buf[i] = 1.0 - 4.0 * wide

    for i in range(R):
        widen_diff(diff[i], i + D)
    loads["pert"].wait()
    loads["incr"].wait()
    loads["m_in"].wait()
    loads["m_out"].wait()
    for n in range(H):
        product = jnp.dot(m_in[n], m_out[n], preferred_element_type=F32)
        both[n] = product.astype(BF16)
        both_t[n] = jnp.transpose(product).astype(BF16)
    loads["obs"].wait()
    loads["innov"].wait()
    loads["prec"].wait()
    step_count = steps_ref[0]

    def put(buf, n, i, value):
        buf[n, i, EDGE:EDGE + LON] = value
        buf[n, i, EDGE - 1:EDGE] = value[LON - 1:LON]
        buf[n, i, EDGE + LON:EDGE + LON + 1] = value[0:1]

    def around(buf, n, i):
        north, south = buf[n, i - 1, EDGE:EDGE + LON], buf[n, i + 1, EDGE:EDGE + LON]
        west, east = buf[n, i, EDGE - 1:EDGE - 1 + LON], buf[n, i, EDGE + 1:EDGE + 1 + LON]
        return (north + south) + (west + east)

    def fwd_row(n, r, value, send=True):
        for s, i in enumerate(pair(r)):
            put(s_buf, n, i + DS, value[s])
        for k in range(H):
            if send and supplied(k) == (n, r + 1):
                if n > 0:
                    for s in range(2):
                        fwd_send[s, k] = value[s].astype(BF16)
                if k in (1, 2, 3):
                    go(jnp.logical_and(has_up, first_core), fwd_up[k])
                    go(jnp.logical_and(has_down, first_core), fwd_down[k])
                else:
                    go(has_up, fwd_up[k])
                    go(has_down, fwd_down[k])

    row = lax.broadcasted_iota(jnp.int32, (GJ, WIDTH), 0)
    lane = lax.broadcasted_iota(jnp.int32, (GJ, WIDTH), 1)
    own_cell = lax.rem(lane, GJ) == row
    groups = LON // GJ

    def places(r):
        found = []
        for at in range(2 * r * LON, 2 * (r + 1) * LON, LANES):
            index = jnp.broadcast_to(cflat[:, at:at + LANES], (MEM, LANES))
            found.append((index // LANES, index % LANES))
        return found

    placed = [places(r) for r in range(HALF)]
    all_here(0, gathered.at[others])
    weights = jnp.concatenate([gathered[p] for p in range(tm_count)], axis=1)
    def pick(r):
        found = []
        for block, inside in placed[r]:
            value = jnp.zeros((MEM, LANES), F32)
            for c in range(C // LANES):
                taken = jnp.take_along_axis(weights[:, c * LANES:(c + 1) * LANES], inside, axis=1)
                value = jnp.where(block == c, taken, value)
            wide = jnp.broadcast_to(value[:, None, :], (MEM, GJ, LANES)).reshape(WIDTH, LANES)
            found.append(jnp.transpose(wide))
        return jnp.concatenate(found, axis=0)

    def begin(r):
        picked = pick(r)
        value = []
        for s, i in enumerate(pair(r)):
            pieces = []
            for g in range(groups):
                at = g * GJ
                block = jnp.where(own_cell, picked[s * LON + at:s * LON + at + GJ], 0.0).astype(BF16)
                members = pert[:, i, at:at + GJ, :].reshape(WIDTH, LEV)
                pieces.append(incr[i, at:at + GJ] + jnp.dot(block, members, preferred_element_type=F32))
            state = jnp.concatenate(pieces, axis=0)
            start[i] = state
            start_bf[i] = state.astype(BF16)
            value.append(state)
        fwd_row(0, r, value)
        go(has_prev, *rows_of(start_back, r))

    def modes(value, both):
        flat = jnp.concatenate([v.astype(BF16) for v in value], axis=0)
        moved = jnp.dot(flat, both, preferred_element_type=F32)
        return [value[s] + moved[s * LON:(s + 1) * LON] for s in range(2)]

    def step(n, r):
        here = [s_buf[n, i + DS, EDGE:EDGE + LON] for i in pair(r)]
        smoothed = [here[s] + d_buf[i + D] * (around(s_buf, n, i + DS) - 4.0 * here[s]) for s, i in enumerate(pair(r))]
        result = modes(smoothed, both[n])
        if n > 0:
            result = [jnp.where(n < step_count, a, b) for a, b in zip(result, here)]
        if n + 1 < H:
            fwd_row(n + 1, r, result)
        else:
            for s, i in enumerate(pair(r)):
                end_buf[i] = result[s]
                end_bf[i] = result[s].astype(BF16)

    def fold(r):
        return R - 1 - r if r >= HALF else r

    def needs_state(n, r, found):
        if (n, r) in found:
            return
        found.add((n, r))
        if n == 0 or (r < 0 and n <= -r - 1):
            return
        for near in (r - 1, r, r + 1):
            needs_state(n - 1, fold(near), found)

    wanted = set()
    for r in range(HALF):
        needs_state(H, r, wanted)
    known = set()

    def forward():
        while True:
            ready = [
                (n, r) for n, r in sorted(wanted) if (n, r) not in known and n > 0
                and not (r < 0 and n <= -r - 1)
                and all((n - 1, fold(q)) in known for q in (r - 1, r, r + 1))
            ]
            if not ready:
                return
            for n, r in ready:
                step(n - 1, r)
                known.add((n, r))

    for r in range(HALF):
        begin(r)
        known.add((0, r))
        if r == max(early):
            for q in late:
                go(has_prev, *rows_of(prec_back, q))
        forward()

    for k in range(H):
        if k in (1, 2, 3):
            go(jnp.logical_and(has_up, second_core), fwd_up[k])
            go(jnp.logical_and(has_down, second_core), fwd_down[k])

    wanted_u, wanted_w = set(), set()

    def needs_u(m, r):
        if (m, r) in wanted_u:
            return
        wanted_u.add((m, r))
        if m == 0 or (r < 0 and m <= -r - 1):
            return
        needs_u(m - 1, r)
        for near in (r - 1, r, r + 1):
            needs_w(m - 1, fold(near))

    def needs_w(m, r):
        if (m, r) in wanted_w:
            return
        wanted_w.add((m, r))
        if not (r < 0 and m <= -r - 1):
            needs_u(m, r)

    for r in range(HALF):
        needs_u(H, r)
    known_u, known_w, coupled_at = set(), set(), set()

    def adj_send_row(k, value):
        for s in range(2):
            adj_send[s, k] = value[s].astype(BF16)
        if k in (2, 3):
            go(jnp.logical_and(has_up, first_core), adj_up[k])
            go(jnp.logical_and(has_down, first_core), adj_down[k])
        else:
            go(has_up, adj_up[k])
            go(has_down, adj_down[k])

    def have_u(m, r, value):
        for s, i in enumerate(pair(r)):
            u_buf[i + D] = value[s]
        known_u.add((m, r))
        for k in range(0, H, 2):
            if r >= 0 and supplied(k) == (m, r + 1):
                adj_send_row(k, value)

    def couple(m, r):
        n = H - 1 - m
        here = [u_buf[i + D] for i in pair(r)]
        coupled = modes(here, both_t[n])
        weighted = [d_buf[i + D] * coupled[s] for s, i in enumerate(pair(r))]
        for s, i in enumerate(pair(r)):
            ec_buf[i + D] = e_buf[i + D] * coupled[s]
            put(w_buf, m, i + DS, weighted[s])
        for k in range(1, H, 2):
            if r >= 0 and supplied(k) == (m, r + 1):
                adj_send_row(k, weighted)

    def settle(m, r):
        value = []
        for s, i in enumerate(pair(r)):
            result = ec_buf[i + D] + around(w_buf, m, i + DS)
            if m < H - 1:
                result = jnp.where(H - 1 - m < step_count, result, u_buf[i + D])
            value.append(result)
        if m + 1 < H:
            have_u(m + 1, r, value)
        else:
            known_u.add((H, r))
            final(r, value)

    level_row = lax.broadcasted_iota(jnp.int32, (MEM * LEV, MEM), 0) // LEV
    level_lane = lax.broadcasted_iota(jnp.int32, (MEM * LEV, MEM), 1)
    own = jnp.where(level_row == level_lane, 1.0, 0.0).astype(BF16)
    copy_row = lax.broadcasted_iota(jnp.int32, (MEM, MEM * GL), 0)
    copy_lane = lax.broadcasted_iota(jnp.int32, (MEM, MEM * GL), 1) // GL
    copies = jnp.where(copy_row == copy_lane, 1.0, 0.0).astype(BF16)
    totals = []

    def final(r, value):
        got(has_prev, (prev_base + r, end_prev.at[pl.ds(0, 2)]))
        terms = []
        for s, i in enumerate(pair(r)):
            total = prec[i].astype(F32) * (start[i] - end_prev[i].astype(F32)) + value[s]
            grad_ref[0, i] = total
            rounded = total.astype(BF16)
            terms.append(jnp.concatenate([pert[k, i] * rounded for k in range(MEM)], axis=1))
        summed = jnp.concatenate([jnp.dot(t, own, preferred_element_type=F32) for t in terms], axis=0)
        spread_cells = jnp.dot(summed.astype(BF16), copies, preferred_element_type=F32).astype(BF16)
        at = 2 * r * LON
        placed_terms = spread_cells * in_lane[at:at + 2 * LON]
        share = jnp.dot(in_group[:, at:at + 2 * LON], placed_terms, preferred_element_type=F32)
        sums_buf[...] = share + sums_buf[...] if totals else share
        totals.append(r)

    def leading(goals):
        need_c, need_s, stack = set(), set(), []
        for m, r in goals:
            stack.append(("c" if (m, r + 1) in [supplied(k) for k in range(1, H, 2)] else "u", m, r))
        while stack:
            kind, m, r = stack.pop()
            if kind == "c" and (m, r) not in need_c:
                need_c.add((m, r))
                stack.append(("u", m, r))
            elif kind == "u" and m > 0 and (m - 1, r) not in need_s:
                need_s.add((m - 1, r))
                stack.extend(("c", m - 1, fold(q)) for q in (r - 1, r, r + 1))
        return need_c, need_s

    def adjoint(goals=None):
        only = leading(goals) if goals else None
        while True:
            ready = [("c", m, r) for m, r in sorted(known_u) if m < H and (m, r) not in coupled_at
                     and ((m, r) in wanted_w or (m + 1, r) in wanted_u)]
            ready += [
                ("s", m - 1, r) for m, r in sorted(wanted_u) if m > 0 and (m, r) not in known_u
                and not (r < 0 and m <= -r - 1) and (m - 1, r) in coupled_at
                and all((m - 1, fold(q)) in known_w for q in (r - 1, r, r + 1))
            ]
            if only:
                ready = [t for t in ready if t[1:] in only[0 if t[0] == "c" else 1]]
            if not ready:
                return
            for kind, m, r in ready:
                if kind == "c":
                    couple(m, r)
                    coupled_at.add((m, r))
                    known_w.add((m, r))
                else:
                    settle(m, r)

    def seed(r):
        value = []
        for i in pair(r):
            end = end_buf[i]
            misfit = obs[i].astype(F32) * (end - innov[i].astype(F32))
            value.append(misfit - prec_next[i].astype(F32) * (start_next[i].astype(F32) - end))
        have_u(0, r, value)

    got(has_down, (2, diff_halo.at[1]))
    got(has_up, (3, diff_halo.at[0]))
    for q in range(1, D + 1):
        widen_diff(diff_halo[0, D - q], D - q)
        widen_diff(diff_halo[1, q - 1], R - 1 + D + q)

    urgent = {(supplied(k)[0], supplied(k)[1] - 1) for k in range(H)}

    def seed_and_send(r):
        got(has_next, (next_base + r, prec_next.at[pl.ds(0, 4)]))
        seed(r)
        adjoint(urgent)

    seeded = []
    for some in early_groups:
        got(has_down, (fwd_sem[some[0]], fwd_recv.at[1, pl.ds(0, len(some))]))
        got(has_up, (fwd_sem[some[0]] + 1, fwd_recv.at[0, pl.ds(0, len(some))]))
        for k in some:
            n, depth = supplied(k)
            fwd_row(n, -depth, [fwd_recv[s, k].astype(F32) for s in range(2)], send=False)
            known.add((n, -depth))
        forward()
        if (H, 1) in known and not seeded:
            seed_and_send(1)
            seeded.append(1)
    for r in range(HALF):
        if r == HALF - 1:
            for q in reversed(range(HALF)):
                go(has_next, *rows_of(end_on, q))
        if r not in seeded:
            seed_and_send(r)
    adjoint()
    for k in range(H):
        if k in (2, 3):
            go(jnp.logical_and(has_up, second_core), adj_up[k])
            go(jnp.logical_and(has_down, second_core), adj_down[k])

    for some in late_groups:
        got(has_down, (adj_sem[some[0]], adj_recv.at[1, pl.ds(0, len(some))]))
        got(has_up, (adj_sem[some[0]] + 1, adj_recv.at[0, pl.ds(0, len(some))]))
        for k in some:
            m, depth = supplied(k)
            value = [adj_recv[s, k].astype(F32) for s in range(2)]
            if k % 2 == 0:
                have_u(m, -depth, value)
            else:
                for s, i in enumerate(pair(-depth)):
                    put(w_buf, m, i + DS, value[s])
                known_w.add((m, -depth))
        adjoint()

    for p in range(tm_count):
        term_send[p] = sums_buf[p * HB:(p + 1) * HB]
    for d in range(1, tm_count):
        term(d).start()
    result = term_send[me_t]
    all_here(1, term_recv.at[others])
    for d in range(1, tm_count):
        result = result + term_recv[lax.rem(me_t + d, tm_count)]
    out_row = lax.broadcasted_iota(jnp.int32, (MEM, LANES), 0)
    out_lane = lax.broadcasted_iota(jnp.int32, (MEM, LANES), 1)
    owned = jnp.zeros((MEM, LANES), F32)
    for b in range(0, MEM * GL, LANES):
        where_from = out_row * GL + lax.rem(out_lane, GL) - b
        inside = (where_from >= 0) & (where_from < LANES)
        where_from = jnp.clip(where_from, 0, LANES - 1)
        for h in range(HB):
            source = jnp.broadcast_to(result[h:h + 1, b:b + LANES], (MEM, LANES))
            taken = jnp.take_along_axis(source, where_from, axis=1)
            owned = jnp.where(inside & (out_lane // GL == h), taken, owned)
    gw_ref[:, 0, :] = owned[:, 0:CW] + gathered[me_t]

    all_sent(0, gathered.at[others])
    all_sent(1, term_send.at[others])
    sent(has_up, (2, diff_halo.at[0]), (7, fwd_send.at[0]), (9, adj_send.at[0]))
    sent(has_down, (3, diff_halo.at[1]), (8, fwd_send.at[1]), (10, adj_send.at[1]))
    sent(has_prev, (4, prec_next), (5, start_next))
    sent(has_next, (6, end_prev))


def deliver(grad, owned, grad_h, gw_h, sem):
    copies = [
        pltpu.make_async_copy(grad, grad_h, sem.at[0]),
        pltpu.make_async_copy(owned, gw_h, sem.at[1]),
    ]
    for copy in copies:
        copy.start()
    for copy in copies:
        copy.wait()


def solution(mesh):
    tm_count, lat_count = mesh.shape["tm"], mesh.shape["lat"]

    def body(incr, pert, weight, cmap, steps, diffusion, m_in, m_out, prec, obs, innov):
        _, R, LON, LEV = incr.shape
        MEM, _, CW = weight.shape
        H = m_in.shape[0]
        D = max(H // 2, 1)
        DS = max(supplied(k)[1] for k in range(H))
        C = CW * tm_count
        GL = min(WIDTH // MEM, CW)
        field = lambda rows, kind: pltpu.VMEM((rows, LON, LEV), kind)
        padded = pltpu.VMEM((H, R + 2 * DS, LON + 2 * EDGE, LEV), F32)
        halo = pltpu.VMEM((2, H, LON, LEV), BF16)
        scratch = [
            field(R, F32),
            pltpu.VMEM((MEM, R, LON, LEV), BF16),
            pltpu.VMEM((tm_count, MEM, CW), F32),
            pltpu.VMEM((R, LON), jnp.int32),
            field(R, BF16),
            pltpu.VMEM((2, D, LON, LEV), BF16),
            field(R + 2 * D, F32), field(R + 2 * D, F32),
            pltpu.VMEM(m_in.shape, BF16),
            pltpu.VMEM(m_out.shape, BF16),
            field(R, BF16), field(R, BF16), field(R, BF16),
            pltpu.VMEM((H, LEV, LEV), BF16),
            pltpu.VMEM((H, LEV, LEV), BF16),
            pltpu.VMEM((1, R * LON), jnp.int32),
            pltpu.VMEM((C // GL, MEM * GL), F32),
            pltpu.VMEM((C // GL, R * LON), BF16),
            pltpu.VMEM((R * LON, MEM * GL), BF16),
            field(R, F32), field(R, BF16), padded, padded,
            field(R + 2 * D, F32), field(R + 2 * D, F32),
            field(R, F32), field(R, BF16), field(R, BF16), field(R, BF16), field(R, BF16),
            halo, halo, halo, halo,
            pltpu.VMEM((tm_count, CW // GL, MEM * GL), F32),
            pltpu.VMEM((tm_count, CW // GL, MEM * GL), F32),
            pltpu.SemaphoreType.DMA((10,)),
            pltpu.SemaphoreType.DMA((11,)),
            pltpu.SemaphoreType.DMA((4 + 2 * min(H, 3) + 2 * (-(-H // 2)) + R,)),
        ]

        def run(*refs):
            kernel(tm_count, lat_count, (H, R, LON, LEV, MEM, CW), *refs)

        fixed = [
            pltpu.with_memory_space_constraint(x, pltpu.HBM)
            for x in (incr, pert, weight, cmap, diffusion, m_in, m_out, prec, obs, innov)
        ]
        grad, owned = pl.pallas_call(
            run,
            out_shape=(
                pltpu.VMEM(incr.shape, F32),
                pltpu.VMEM((MEM, 1, CW), F32),
            ),
            in_specs=[pl.BlockSpec(memory_space=pltpu.SMEM)] + [pl.BlockSpec(memory_space=pltpu.HBM)] * 10,
            out_specs=(pl.BlockSpec(memory_space=pltpu.VMEM), pl.BlockSpec(memory_space=pltpu.VMEM)),
            scratch_shapes=scratch,
            compiler_params=pltpu.CompilerParams(
                collective_id=0, has_side_effects=True, vmem_limit_bytes=48 * 1024 * 1024
            ),
        )(steps, *fixed)
        grad = pltpu.with_memory_space_constraint(grad, pltpu.VMEM)
        owned = pltpu.with_memory_space_constraint(owned, pltpu.VMEM)
        return pl.pallas_call(
            deliver,
            out_shape=(
                jax.ShapeDtypeStruct(incr.shape, F32),
                jax.ShapeDtypeStruct((MEM, 1, CW), F32),
            ),
            in_specs=[pl.BlockSpec(memory_space=pltpu.VMEM)] * 2,
            out_specs=(pl.BlockSpec(memory_space=pl.ANY), pl.BlockSpec(memory_space=pl.ANY)),
            scratch_shapes=[pltpu.SemaphoreType.DMA((2,))],
        )(grad, owned)

    return jax.shard_map(
        body,
        mesh=mesh,
        in_specs=(
            P("tm", "lat", None, None),
            P(None, "tm", "lat", None, None),
            P(None, "lat", "tm"),
            P("lat", None),
            P("tm"),
            P("tm", "lat", None, None),
            P(),
            P(),
            P("tm", "lat", None, None),
            P("tm", "lat", None, None),
            P("tm", "lat", None, None),
        ),
        out_specs=(P("tm", "lat", None, None), P(None, "lat", "tm")),
        check_vma=False,
    )
```
